32 devices in a mesh: grp: 2 (over y), src: 8 (over z, x), tgt: 2 (over core).
Axes of the slice: x: 2, y: 2, z: 4, core: 2. Of those that a mesh axis runs over, the one named last changes fastest.
Arguments:
- source_feat: float32 [256, 64, 128], P(('grp', 'src')), parts along dimension 0, may hold values from -1.2 to 1.2
- target_feat: float32 [32, 64, 128], P(('grp', 'src', 'tgt')), parts along dimension 0, may hold values from -1.2 to 1.2
- log_mass_src: float32 [256, 128], P(('grp', 'src')), parts along dimension 0, may hold values from -3 to 3
- log_mass_tgt: float32 [32, 128], P(('grp', 'src', 'tgt')), parts along dimension 0, may hold values from -3 to 3
- potential_tgt: float32 [32, 128], P(('grp', 'src', 'tgt')), parts along dimension 0, may hold values from -6 to 152
- support: int32 [256, 2, 8], P(('grp', 'src'), 'tgt'), parts along dimension 0, may hold values from 0 to 7, as said below
- counts: int32 [256, 2], P(('grp', 'src'), 'tgt'), parts along dimension 0, may hold values from 1 to 8, as said below
Outputs:
- potential_src: float32 [256, 128], P(('grp', 'src')), parts along dimension 0
- potential_new: float32 [32, 128], P(('grp', 'src', 'tgt')), parts along dimension 0
The draws below stay inside these ranges and needn't reach their ends.
There are 2 independent parts, one for each index of `grp`. The reference program is written for one: setup_inputs(seed, part) draws one part's arguments, and reference() takes and returns one part's arrays. A program takes and returns all parts, laid end to end along the dimension named above; each array names one. Nothing has to cross between parts.
Inputs may be any that keep to these rules, and one draw needn't show every extreme that they name: `support`: within one list the first counts entries are distinct; unused entries are also valid indices and are ignored; every target block of a shard is named within the used entries of some source block row. `counts`: the source block rows of one index of src share a load level, so some devices use far more slots than others; some list is full in every draw.
All inputs are finite; a program needn't handle non-finite values.
Results may differ from the reference program's by a relative error of at most 0.000096.
Values sent between devices are 32-bit elements; how exact they have to be, the bound alone decides.
A program may use at most 64 MiB of HBM per device.

```python
import math
import jax
import jax.numpy as jnp
from jax import lax

F = 64
BLOCK = 128
KT = 8
RB = 16
NSB = 128
TBD = 8
NTB = 16


def feature_draw(key, shape):
    second = jax.random.fold_in(key, 1)
    values = 0.3 * jax.random.normal(second, shape)
    return jnp.clip(values, -1.2, 1.2).astype(jnp.float32)


def draw_source_feat(key, part):
    return feature_draw(jax.random.fold_in(key, 11), (NSB, F, BLOCK))


def draw_target_feat(key, part):
    return feature_draw(jax.random.fold_in(key, 23), (NTB, F, BLOCK))


def draw_potential_tgt(key, part):
    first = jax.random.fold_in(jax.random.fold_in(key, 71), 0)
    values = jnp.clip(jax.random.normal(first, (NTB, BLOCK)), -6.0, 6.0)
    return values.astype(jnp.float32)


def draw_support(key, part):
    shards = NTB // TBD
    lists = NSB * shards
    keys = jax.random.split(jax.random.fold_in(key, 37), lists)
    offsets = jax.vmap(lambda single: jax.random.permutation(single, TBD - 1))(keys) + 1
    slot_offsets = jnp.concatenate([jnp.zeros((lists, 1), jnp.int32), offsets[:, :KT - 1].astype(jnp.int32)], axis=1)
    base_rows = jnp.arange(lists, dtype=jnp.int32) // shards % TBD
    chosen = (base_rows[:, None] + slot_offsets) % TBD
    return chosen.reshape(NSB, shards, KT).astype(jnp.int32)


def draw_counts(key, part):
    shards = NTB // TBD
    first, second = jax.random.split(jax.random.fold_in(key, 53))
    levels = jax.random.randint(first, (NSB // RB,), 1, KT + 1)
    level_rows = jnp.repeat(levels, RB)
    drawn = jax.random.randint(second, (NSB, shards), 1, KT + 1)
    drawn = jnp.minimum(drawn, level_rows[:, None])
    drawn = drawn.at[0, 0].set(KT)
    return drawn.astype(jnp.int32)


def block_levels(rng, shape, cuts, least, high):
    def one(dim, shards_of):
        heights = jax.random.uniform(jax.random.fold_in(jax.random.fold_in(rng, 6), dim), (shards_of,), jnp.float32, least / len(cuts), high / len(cuts))
        return jnp.repeat(jnp.exp(heights), shape[dim] // shards_of).reshape((-1,) + (1,) * (len(shape) - dim - 1))

    factor_of = one(*cuts[0])
    for cut in cuts[1:]:
        factor_of = factor_of * one(*cut)
    return factor_of


def setup_inputs(seed: int = 0, part: int = 0) -> dict:
    seeds = jax.random.split(jax.random.key(seed), 8)
    own_keys = jax.random.split(jax.random.fold_in(seeds[7], part), 8)
    source_feat = draw_source_feat(jax.random.fold_in(jax.random.fold_in(seeds[7], part), 71), part)
    target_feat = draw_target_feat(jax.random.fold_in(jax.random.fold_in(seeds[7], part), 71), part)
    log_mass_src = jnp.clip(jax.random.uniform(own_keys[2], (NSB, BLOCK), jnp.float32, -3.0, 3.0) * block_levels(own_keys[2], (NSB, BLOCK), ((0, 8),), -0.4, 0.0), -3.0, 3.0)
    log_mass_tgt = jnp.clip(jax.random.uniform(own_keys[3], (NTB, BLOCK), jnp.float32, -3.0, 3.0) * block_levels(own_keys[3], (NTB, BLOCK), ((0, 16),), -0.4, 0.0), -3.0, 3.0)
    potential_tgt = draw_potential_tgt(jax.random.fold_in(jax.random.fold_in(seeds[7], part), 71), part)
    support = draw_support(jax.random.fold_in(jax.random.fold_in(seeds[7], part), 71), part)
    counts = draw_counts(jax.random.fold_in(jax.random.fold_in(seeds[7], part), 71), part)
    return {"source_feat": source_feat, "target_feat": target_feat, "log_mass_src": log_mass_src, "log_mass_tgt": log_mass_tgt, "potential_tgt": potential_tgt, "support": support, "counts": counts}


entropic = 0.5
very_low = -1.0e30


def cost_tiles(source_blk, source_sq, target_blk, target_sq):
    cross = jnp.einsum("...fi,...fj->...ij", source_blk, target_blk, precision=lax.Precision.HIGHEST)
    return source_sq[..., :, None] + target_sq[..., None, :] - 2.0 * cross


def row_stats(cost, mass_tgt, poten_tgt, usable):
    scores = mass_tgt[..., None, :] + (poten_tgt[..., None, :] - cost) / entropic
    scores = jnp.where(usable[..., None, None], scores, very_low)
    peak = jnp.max(scores, axis=(1, 3))
    total = jnp.sum(jnp.exp(scores - peak[:, None, :, None]), axis=(1, 3))
    return peak, total


def column_stats(cost, mass_src, poten_src, usable):
    scores = mass_src[:, None, :, None] + (poten_src[:, None, :, None] - cost) / entropic
    peak = jnp.max(scores, axis=2)
    total = jnp.sum(jnp.exp(scores - peak[:, :, None, :]), axis=2)
    peak = jnp.where(usable[..., None], peak, very_low)
    total = jnp.where(usable[..., None], total, 0.0)
    return peak, total


def segment_merge(peaks, totals, seg_ids, segments):
    best = jax.ops.segment_max(peaks, seg_ids, num_segments=segments + 1)
    best = jnp.maximum(best, very_low)
    summed = jax.ops.segment_sum(totals * jnp.exp(peaks - best[seg_ids]), seg_ids, num_segments=segments + 1)
    return best[:segments], summed[:segments]


def reference(source_feat, target_feat, log_mass_src, log_mass_tgt, potential_tgt, support, counts):
    shards = NTB // TBD

    def regroup(array):
        split = array.reshape((TBD, shards) + array.shape[1:])
        return jnp.swapaxes(split, 0, 1).reshape((NTB,) + array.shape[1:])

    target_all = regroup(target_feat)
    mass_all = regroup(log_mass_tgt)
    poten_all = regroup(potential_tgt)
    target_sq = jnp.sum(target_all * target_all, axis=1)
    source_sq = jnp.sum(source_feat * source_feat, axis=1)
    offsets = (jnp.arange(shards, dtype=jnp.int32) * TBD)[None, :, None]
    block_ids = (support + offsets).reshape(NSB, shards * KT)
    usable = (jnp.arange(KT, dtype=jnp.int32)[None, None, :] < counts[:, :, None]).reshape(NSB, shards * KT)
    width = math.gcd(NSB, 8)

    def grouped(array):
        return array.reshape((NSB // width, width) + array.shape[1:])

    def row_pass(items):
        source_blk, source_nrm, ids_here, use_here = items
        cost = cost_tiles(source_blk[:, None], source_nrm[:, None], target_all[ids_here], target_sq[ids_here])
        return row_stats(cost, mass_all[ids_here], poten_all[ids_here], use_here)

    peak, total = lax.map(row_pass, (grouped(source_feat), grouped(source_sq), grouped(block_ids), grouped(usable)))
    potential_src = (-entropic * (peak + jnp.log(total))).reshape(NSB, BLOCK)

    def column_pass(items):
        source_blk, source_nrm, mass_here, poten_here, ids_here, use_here = items
        cost = cost_tiles(source_blk[:, None], source_nrm[:, None], target_all[ids_here], target_sq[ids_here])
        return column_stats(cost, mass_here, poten_here, use_here)

    peaks, totals = lax.map(column_pass, (grouped(source_feat), grouped(source_sq), grouped(log_mass_src), grouped(potential_src), grouped(block_ids), grouped(usable)))
    seg_ids = jnp.where(usable, block_ids, NTB).reshape(-1)
    best, summed = segment_merge(peaks.reshape(-1, BLOCK), totals.reshape(-1, BLOCK), seg_ids, NTB)
    updated = -entropic * (best + jnp.log(summed))
    potential_new = jnp.swapaxes(updated.reshape(shards, TBD, BLOCK), 0, 1).reshape(NTB, BLOCK)
    return potential_src, potential_new
```

```python
import functools
import math

import jax
import jax.numpy as jnp
from jax import lax
from jax.experimental import pallas as pl
from jax.experimental.pallas import tpu as pltpu
from jax.sharding import PartitionSpec as P

entropic = 0.5
very_low = -1e30


def merged(part, axis, combine):
    gathered = jax.tree.map(lambda a: lax.all_gather(a, axis), part)

    def take(source):
        return jax.tree.map(lambda a: lax.dynamic_index_in_dim(a, source, 0, False), gathered)

    return lax.fori_loop(
        1, lax.axis_size(axis), lambda source, state: combine(state, take(source)), take(0)
    )


def cost_tiles(source_blk, source_sq, target_blk, target_sq):
    cross = jnp.einsum(
        "...fi,...fj->...ij", source_blk, target_blk, precision=lax.Precision.HIGHEST
    )
    return source_sq[..., :, None] + target_sq[..., None, :] - 2.0 * cross


def row_stats(cost, mass_tgt, poten_tgt, usable):
    scores = mass_tgt[..., None, :] + (poten_tgt[..., None, :] - cost) / entropic
    scores = jnp.where(usable[..., None, None], scores, very_low)
    peak = jnp.max(scores, axis=(1, 3))
    total = jnp.sum(jnp.exp(scores - peak[:, None, :, None]), axis=(1, 3))
    return (peak, total)


def column_stats(cost, mass_src, poten_src, usable):
    scores = mass_src[:, None, :, None] + (poten_src[:, None, :, None] - cost) / entropic
    peak = jnp.max(scores, axis=2)
    total = jnp.sum(jnp.exp(scores - peak[:, :, None, :]), axis=2)
    peak = jnp.where(usable[..., None], peak, very_low)
    total = jnp.where(usable[..., None], total, 0.0)
    return (peak, total)


def merge_pair(first_pair, second_pair):
    first_peak, first_total = first_pair
    second_peak, second_total = second_pair
    highest = jnp.maximum(first_peak, second_peak)
    summed = first_total * jnp.exp(first_peak - highest) + second_total * jnp.exp(
        second_peak - highest
    )
    return (highest, summed)


def segment_merge(peaks, totals, seg_ids, segments):
    best = jax.ops.segment_max(peaks, seg_ids, num_segments=segments + 1)
    best = jnp.maximum(best, very_low)
    summed = jax.ops.segment_sum(
        totals * jnp.exp(peaks - best[seg_ids]), seg_ids, num_segments=segments + 1
    )
    return (best[:segments], summed[:segments])


def general_path(
    source_feat, target_feat, log_mass_src, log_mass_tgt, potential_tgt, support, counts
):
    target_all, mass_all, poten_all = (
        lax.all_gather(target_feat, "src", axis=0, tiled=True),
        lax.all_gather(log_mass_tgt, "src", axis=0, tiled=True),
        lax.all_gather(potential_tgt, "src", axis=0, tiled=True),
    )
    blocks = target_all.shape[0]
    rows_here = source_feat.shape[0]
    slots_here = support.shape[2]
    cells = source_feat.shape[2]
    indices = support[:, 0, :]
    limits = counts[:, 0]
    usable = jnp.arange(slots_here, dtype=jnp.int32)[None, :] < limits[:, None]
    source_sq = jnp.sum(source_feat * source_feat, axis=1)
    target_sq = jnp.sum(target_all * target_all, axis=1)
    width = math.gcd(rows_here, 4)

    def grouped(array):
        return array.reshape((rows_here // width, width) + array.shape[1:])

    def row_pass(items):
        source_blk, source_nrm, ids_here, use_here = items
        cost = cost_tiles(
            source_blk[:, None], source_nrm[:, None], target_all[ids_here], target_sq[ids_here]
        )
        return row_stats(cost, mass_all[ids_here], poten_all[ids_here], use_here)

    peak, total = lax.map(
        row_pass, (grouped(source_feat), grouped(source_sq), grouped(indices), grouped(usable))
    )
    peak = peak.reshape(rows_here, cells)
    total = total.reshape(rows_here, cells)
    peak_all, total_all = merged((peak, total), "tgt", merge_pair)
    potential_src = -entropic * (peak_all + jnp.log(total_all))

    def column_pass(items):
        source_blk, source_nrm, mass_here, poten_here, ids_here, use_here = items
        cost = cost_tiles(
            source_blk[:, None], source_nrm[:, None], target_all[ids_here], target_sq[ids_here]
        )
        return column_stats(cost, mass_here, poten_here, use_here)

    peaks, totals = lax.map(
        column_pass,
        (
            grouped(source_feat),
            grouped(source_sq),
            grouped(log_mass_src),
            grouped(potential_src),
            grouped(indices),
            grouped(usable),
        ),
    )
    seg_ids = jnp.where(usable, indices, blocks).reshape(-1)
    best, summed = segment_merge(
        peaks.reshape(-1, cells), totals.reshape(-1, cells), seg_ids, blocks
    )
    share = blocks // lax.axis_size("src")
    own_start = lax.axis_index("src") * share
    highest = lax.pmax(best, "src")
    whole = lax.psum(summed * jnp.exp(best - highest), "src")
    own_peak = lax.dynamic_slice_in_dim(highest, own_start, share, 0)
    own_total = lax.dynamic_slice_in_dim(whole, own_start, share, 0)
    potential_new = -entropic * (own_peak + jnp.log(own_total))
    return (potential_src, potential_new)


LOG2E = 1.4426950408889634
LN2 = 0.6931471805599453
MESH = pl.DeviceIdType.MESH
DENSE_BYTES = 24 * 1024 * 1024


def split3(value):
    high = value.astype(jnp.bfloat16).astype(jnp.float32)
    rest = value - high
    mid = rest.astype(jnp.bfloat16).astype(jnp.float32)
    return high, mid, rest - mid


def partner(me, step, count):
    if count & (count - 1):
        return (me + step) % count
    met, bit = 0, 1
    while bit < count:
        met = met + bit * ((me // bit + step // bit) % 2)
        bit *= 2
    return met


def origin(me, step, count):
    if count & (count - 1):
        return (me - step + count) % count
    return partner(me, step, count)


def sinkhorn_kernel(
    n_src, n_tgt, chunk,
    x_ref, y_ref, lms_ref, lmt_ref, pt_ref, sup_ref, cnt_ref,
    ps_ref, pn_ref,
    y_all, lm_all, pt_all, xt, scores, run_max, bias, peak_col, total_col, shift,
    x_sq, stat_out, stat_in, col_out, col_in,
    y_send, y_recv, s_send, s_recv, c_send, c_recv,
):
    rows, feats, cells = x_ref.shape
    slots = sup_ref.shape[2]
    grp = lax.axis_index("grp")
    me = lax.axis_index("src")
    shard = lax.axis_index("tgt")

    barrier = pltpu.get_barrier_semaphore()
    for step in range(1, n_src):
        pl.semaphore_signal(
            barrier, inc=1, device_id=(grp, partner(me, step, n_src), shard), device_id_type=MESH
        )
    for step in range(1, n_tgt):
        pl.semaphore_signal(
            barrier, inc=1, device_id=(grp, me, (shard + step) % n_tgt), device_id_type=MESH
        )
    pl.semaphore_wait(barrier, n_src - 1 + n_tgt - 1)

    parts = ((y_ref, y_all), (lmt_ref, lm_all), (pt_ref, pt_all))

    def target_copy(index, where, step, peer):
        mine, everyone = parts[index]
        return pltpu.make_async_remote_copy(
            src_ref=mine,
            dst_ref=everyone.at[pl.ds(where, 1)],
            send_sem=y_send.at[index, step],
            recv_sem=y_recv.at[index, where],
            device_id=(grp, peer, shard),
            device_id_type=MESH,
        )

    for step in range(1, n_src):
        peer = partner(me, step, n_src)
        for index in range(3):
            target_copy(index, me, step, peer).start()
    y_all[me] = y_ref[0]
    lm_all[pl.ds(me, 1)] = lmt_ref[...]
    pt_all[pl.ds(me, 1)] = pt_ref[...]

    def prepare(row, carry):
        x = x_ref[row]
        x_sq[pl.ds(row, 1)] = jnp.sum(x * x, axis=0, keepdims=True)
        high, mid, low = split3(x * (4.0 * LOG2E))
        first = jnp.concatenate([high, mid], axis=0).T.astype(jnp.bfloat16)
        second = jnp.concatenate([low, high], axis=0).T.astype(jnp.bfloat16)
        here = pl.ds(row * cells, cells)
        xt[here, 0 : 2 * feats] = first
        xt[here, 2 * feats : 4 * feats] = first
        xt[here, 4 * feats : 6 * feats] = second
        return carry

    lax.fori_loop(0, rows, prepare, 0)
    run_max[...] = jnp.full(run_max.shape, 4.0 * very_low, jnp.float32)

    limits = cnt_ref[...]
    ids = sup_ref[:, 0, :]

    def block_scores(block):
        y = y_all[block]
        high, mid, low = split3(y)
        weights = jnp.concatenate([high, high, mid, mid, high, low], axis=0).astype(jnp.bfloat16)
        y_sq = jnp.sum(y * y, axis=0, keepdims=True)
        level = LOG2E * (
            lm_all[pl.ds(block, 1)] + 2.0 * pt_all[pl.ds(block, 1)] - 2.0 * y_sq
        )
        joined = jnp.zeros((rows, 1), jnp.bool_)
        for slot in range(slots):
            joined = joined | ((ids[:, slot : slot + 1] == block) & (limits > slot))
        bias[...] = level + jnp.where(joined, 0.0, very_low)
        for start in range(0, rows, chunk):
            here = slice(start * cells, (start + chunk) * cells)
            cross = jnp.dot(xt[here, :], weights, preferred_element_type=jnp.float32)
            for row in range(chunk):
                tile = slice((start + row) * cells, (start + row + 1) * cells)
                value = cross[row * cells : (row + 1) * cells] + bias[start + row : start + row + 1]
                scores[block, tile] = value
                run_max[tile] = jnp.maximum(run_max[tile], value)

    block_scores(me)

    def arrival(step, carry):
        block = origin(me, step, n_src)
        for index in range(3):
            target_copy(index, block, step, block).wait_recv()
        block_scores(block)
        return carry

    lax.fori_loop(1, n_src, arrival, 0)

    lanes = lax.broadcasted_iota(jnp.int32, (cells, cells), 1)
    peak_col[...] = jnp.zeros_like(peak_col)
    total_col[...] = jnp.ones_like(total_col)

    def row_block(row, carry):
        here = pl.ds(row * cells, cells)
        peak = jnp.max(run_max[here], axis=1, keepdims=True)
        gathered = jnp.exp2(scores[0, here] - peak)
        for block in range(1, n_src):
            gathered = gathered + jnp.exp2(scores[block, here] - peak)
        total = jnp.sum(gathered, axis=1, keepdims=True)
        chosen = lanes == row
        peak_col[...] = jnp.where(chosen, peak, peak_col[...])
        total_col[...] = jnp.where(chosen, total, total_col[...])
        return carry

    lax.fori_loop(0, rows, row_block, 0)
    own_peak = peak_col[...].T[:rows]
    own_total = total_col[...].T[:rows]
    stat_out[0] = own_peak
    stat_out[1] = own_total

    def stat_copy(where, step, peer):
        return pltpu.make_async_remote_copy(
            src_ref=stat_out,
            dst_ref=stat_in.at[where],
            send_sem=s_send.at[step],
            recv_sem=s_recv.at[where],
            device_id=(grp, me, peer),
            device_id_type=MESH,
        )

    for step in range(1, n_tgt):
        stat_copy(step, step, (shard + step) % n_tgt).start()
    for step in range(1, n_src):
        for index in range(3):
            target_copy(index, me, step, partner(me, step, n_src)).wait_send()
    for step in range(1, n_tgt):
        stat_copy(step, step, (shard + step) % n_tgt).wait_recv()
    peak, total = own_peak, own_total
    for step in range(1, n_tgt):
        other_peak, other_total = stat_in[step, 0], stat_in[step, 1]
        highest = jnp.maximum(peak, other_peak)
        total = total * jnp.exp2(peak - highest) + other_total * jnp.exp2(other_peak - highest)
        peak = highest
    joint = peak + jnp.log(total) * LOG2E
    ps_ref[...] = x_sq[...] - (entropic * LN2) * joint
    offset = LOG2E * lms_ref[...] - joint
    offset = jnp.concatenate([offset, jnp.zeros((cells - rows, cells), jnp.float32)], axis=0).T
    for row in range(rows):
        shift[row * cells : (row + 1) * cells] = jnp.broadcast_to(
            offset[:, row : row + 1], (cells, cells)
        )

    def column(block):
        def highest(row, best):
            here = pl.ds(row * cells, cells)
            value = scores[block, here] + shift[here]
            scores[block, here] = value
            return jnp.maximum(best, jnp.max(value.reshape(cells // 8, 8, cells), axis=0))

        best = lax.fori_loop(0, rows, highest, jnp.full((8, cells), 4.0 * very_low, jnp.float32))
        best = jnp.max(best, axis=0, keepdims=True)

        def add(row, summed):
            here = pl.ds(row * cells, cells)
            value = jnp.exp2(scores[block, here] - best)
            return summed + jnp.sum(value.reshape(cells // 8, 8, cells), axis=0)

        summed = lax.fori_loop(0, rows, add, jnp.zeros((8, cells), jnp.float32))
        return best, jnp.sum(summed, axis=0, keepdims=True)

    def column_copy(dest, where, step):
        return pltpu.make_async_remote_copy(
            src_ref=col_out.at[dest],
            dst_ref=col_in.at[where],
            send_sem=c_send.at[step],
            recv_sem=c_recv.at[where],
            device_id=(grp, dest, shard),
            device_id_type=MESH,
        )

    def send_column(index, carry):
        step = n_src - 1 - index
        block = partner(me, step, n_src)
        best, summed = column(block)
        col_out[block, 0:1] = best
        col_out[block, 1:2] = summed
        column_copy(block, me, step).start()
        return carry

    lax.fori_loop(0, n_src - 1, send_column, 0)
    best, summed = column(me)
    col_in[me, 0:1] = best
    col_in[me, 1:2] = summed
    for step in range(1, n_src):
        sender = origin(me, step, n_src)
        column_copy(sender, sender, step).wait_recv()
    peaks = col_in[:, 0, :]
    totals = col_in[:, 1, :]
    highest = jnp.max(peaks, axis=0, keepdims=True)
    whole = jnp.sum(totals * jnp.exp2(peaks - highest), axis=0, keepdims=True)
    pn_ref[...] = (
        pt_ref[...]
        + entropic * lmt_ref[...]
        - (entropic * LN2) * (highest + jnp.log(whole) * LOG2E)
    )
    for step in range(1, n_tgt):
        stat_copy(step, step, (shard + step) % n_tgt).wait_send()
    for step in range(1, n_src):
        column_copy(partner(me, step, n_src), me, step).wait_send()


def dense_path(source_feat, target_feat, log_mass_src, log_mass_tgt, potential_tgt, support, counts):
    n_src, n_tgt = lax.axis_size("src"), lax.axis_size("tgt")
    rows, feats, cells = source_feat.shape
    vmem = pl.BlockSpec(memory_space=pltpu.VMEM)
    f32 = jnp.float32
    dma = pltpu.SemaphoreType.DMA
    return pl.pallas_call(
        functools.partial(sinkhorn_kernel, n_src, n_tgt, math.gcd(rows, 4)),
        out_shape=(
            jax.ShapeDtypeStruct((rows, cells), f32),
            jax.ShapeDtypeStruct((1, cells), f32),
        ),
        in_specs=[vmem] * 7,
        out_specs=(vmem, vmem),
        scratch_shapes=[
            pltpu.VMEM((n_src, feats, cells), f32),
            pltpu.VMEM((n_src, cells), f32),
            pltpu.VMEM((n_src, cells), f32),
            pltpu.VMEM((rows * cells, 6 * feats), jnp.bfloat16),
            pltpu.VMEM((n_src, rows * cells, cells), f32),
            pltpu.VMEM((rows * cells, cells), f32),
            pltpu.VMEM((rows, cells), f32),
            pltpu.VMEM((cells, cells), f32),
            pltpu.VMEM((cells, cells), f32),
            pltpu.VMEM((rows * cells, cells), f32),
            pltpu.VMEM((rows, cells), f32),
            pltpu.VMEM((2, rows, cells), f32),
            pltpu.VMEM((n_tgt, 2, rows, cells), f32),
            pltpu.VMEM((n_src, 2, cells), f32),
            pltpu.VMEM((n_src, 2, cells), f32),
            dma((3, n_src)),
            dma((3, n_src)),
            dma((n_tgt,)),
            dma((n_tgt,)),
            dma((n_src,)),
            dma((n_src,)),
        ],
        compiler_params=pltpu.CompilerParams(
            collective_id=0, has_side_effects=True, vmem_limit_bytes=48 * 1024 * 1024
        ),
        name="sinkhorn",
    )(source_feat, target_feat, log_mass_src, log_mass_tgt, potential_tgt, support, counts)


def per_device(
    source_feat, target_feat, log_mass_src, log_mass_tgt, potential_tgt, support, counts
):
    rows, feats, cells = source_feat.shape
    n_src = lax.axis_size("src")
    dense = 4 * n_src * rows * cells * cells
    fits = (
        dense <= DENSE_BYTES
        and target_feat.shape[0] == 1
        and cells % 128 == 0
        and rows <= cells
        and 2 * feats == cells
        and n_src % 8 == 0
        and rows % 8 == 0
    )
    path = dense_path if fits else general_path
    return path(
        source_feat, target_feat, log_mass_src, log_mass_tgt, potential_tgt, support, counts
    )


def solution(mesh):
    in_specs = (
        P(("grp", "src"), None, None),
        P(("grp", "src", "tgt"), None, None),
        P(("grp", "src"), None),
        P(("grp", "src", "tgt"), None),
        P(("grp", "src", "tgt"), None),
        P(("grp", "src"), "tgt", None),
        P(("grp", "src"), "tgt"),
    )
    out_specs = (P(("grp", "src"), None), P(("grp", "src", "tgt"), None))
    return jax.shard_map(
        per_device, mesh=mesh, in_specs=in_specs, out_specs=out_specs, check_vma=False
    )
```

```python
import functools
import math

import jax
import jax.numpy as jnp
from jax import lax
from jax.experimental import pallas as pl
from jax.experimental.pallas import tpu as pltpu
from jax.sharding import PartitionSpec as P

entropic = 0.5
very_low = -1e30


def merged(part, axis, combine):
    gathered = jax.tree.map(lambda a: lax.all_gather(a, axis), part)

    def take(source):
        return jax.tree.map(lambda a: lax.dynamic_index_in_dim(a, source, 0, False), gathered)

    return lax.fori_loop(
        1, lax.axis_size(axis), lambda source, state: combine(state, take(source)), take(0)
    )


def cost_tiles(source_blk, source_sq, target_blk, target_sq):
    cross = jnp.einsum(
        "...fi,...fj->...ij", source_blk, target_blk, precision=lax.Precision.HIGHEST
    )
    return source_sq[..., :, None] + target_sq[..., None, :] - 2.0 * cross


def row_stats(cost, mass_tgt, poten_tgt, usable):
    scores = mass_tgt[..., None, :] + (poten_tgt[..., None, :] - cost) / entropic
    scores = jnp.where(usable[..., None, None], scores, very_low)
    peak = jnp.max(scores, axis=(1, 3))
    total = jnp.sum(jnp.exp(scores - peak[:, None, :, None]), axis=(1, 3))
    return (peak, total)


def column_stats(cost, mass_src, poten_src, usable):
    scores = mass_src[:, None, :, None] + (poten_src[:, None, :, None] - cost) / entropic
    peak = jnp.max(scores, axis=2)
    total = jnp.sum(jnp.exp(scores - peak[:, :, None, :]), axis=2)
    peak = jnp.where(usable[..., None], peak, very_low)
    total = jnp.where(usable[..., None], total, 0.0)
    return (peak, total)


def merge_pair(first_pair, second_pair):
    first_peak, first_total = first_pair
    second_peak, second_total = second_pair
    highest = jnp.maximum(first_peak, second_peak)
    summed = first_total * jnp.exp(first_peak - highest) + second_total * jnp.exp(
        second_peak - highest
    )
    return (highest, summed)


def segment_merge(peaks, totals, seg_ids, segments):
    best = jax.ops.segment_max(peaks, seg_ids, num_segments=segments + 1)
    best = jnp.maximum(best, very_low)
    summed = jax.ops.segment_sum(
        totals * jnp.exp(peaks - best[seg_ids]), seg_ids, num_segments=segments + 1
    )
    return (best[:segments], summed[:segments])


def general_path(
    source_feat, target_feat, log_mass_src, log_mass_tgt, potential_tgt, support, counts
):
    target_all, mass_all, poten_all = (
        lax.all_gather(target_feat, "src", axis=0, tiled=True),
        lax.all_gather(log_mass_tgt, "src", axis=0, tiled=True),
        lax.all_gather(potential_tgt, "src", axis=0, tiled=True),
    )
    blocks = target_all.shape[0]
    rows_here = source_feat.shape[0]
    slots_here = support.shape[2]
    cells = source_feat.shape[2]
    indices = support[:, 0, :]
    limits = counts[:, 0]
    usable = jnp.arange(slots_here, dtype=jnp.int32)[None, :] < limits[:, None]
    source_sq = jnp.sum(source_feat * source_feat, axis=1)
    target_sq = jnp.sum(target_all * target_all, axis=1)
    width = math.gcd(rows_here, 4)

    def grouped(array):
        return array.reshape((rows_here // width, width) + array.shape[1:])

    def row_pass(items):
        source_blk, source_nrm, ids_here, use_here = items
        cost = cost_tiles(
            source_blk[:, None], source_nrm[:, None], target_all[ids_here], target_sq[ids_here]
        )
        return row_stats(cost, mass_all[ids_here], poten_all[ids_here], use_here)

    peak, total = lax.map(
        row_pass, (grouped(source_feat), grouped(source_sq), grouped(indices), grouped(usable))
    )
    peak = peak.reshape(rows_here, cells)
    total = total.reshape(rows_here, cells)
    peak_all, total_all = merged((peak, total), "tgt", merge_pair)
    potential_src = -entropic * (peak_all + jnp.log(total_all))

    def column_pass(items):
        source_blk, source_nrm, mass_here, poten_here, ids_here, use_here = items
        cost = cost_tiles(
            source_blk[:, None], source_nrm[:, None], target_all[ids_here], target_sq[ids_here]
        )
        return column_stats(cost, mass_here, poten_here, use_here)

    peaks, totals = lax.map(
        column_pass,
        (
            grouped(source_feat),
            grouped(source_sq),
            grouped(log_mass_src),
            grouped(potential_src),
            grouped(indices),
            grouped(usable),
        ),
    )
    seg_ids = jnp.where(usable, indices, blocks).reshape(-1)
    best, summed = segment_merge(
        peaks.reshape(-1, cells), totals.reshape(-1, cells), seg_ids, blocks
    )
    share = blocks // lax.axis_size("src")
    own_start = lax.axis_index("src") * share
    highest = lax.pmax(best, "src")
    whole = lax.psum(summed * jnp.exp(best - highest), "src")
    own_peak = lax.dynamic_slice_in_dim(highest, own_start, share, 0)
    own_total = lax.dynamic_slice_in_dim(whole, own_start, share, 0)
    potential_new = -entropic * (own_peak + jnp.log(own_total))
    return (potential_src, potential_new)


LOG2E = 1.4426950408889634
LN2 = 0.6931471805599453
MESH = pl.DeviceIdType.MESH
DENSE_BYTES = 24 * 1024 * 1024


def split3(value):
    high = value.astype(jnp.bfloat16).astype(jnp.float32)
    rest = value - high
    mid = rest.astype(jnp.bfloat16).astype(jnp.float32)
    return high, mid, rest - mid


def partner(me, step, count):
    if count & (count - 1):
        return (me + step) % count
    met, bit = 0, 1
    while bit < count:
        met = met + bit * ((me // bit + step // bit) % 2)
        bit *= 2
    return met


def origin(me, step, count):
    if count & (count - 1):
        return (me - step + count) % count
    return partner(me, step, count)


def sinkhorn_kernel(
    n_src, n_tgt, group,
    x_hbm, y_hbm, lms_hbm, lmt_hbm, pt_hbm, sup_hbm, cnt_hbm,
    ps_ref, pn_ref,
    x_ref, lms_ref, sup_ref, cnt_ref,
    y_all, lm_all, pt_all, xt, scores, run_max, square, used, stat_col, shift,
    x_sq, stat_out, stat_in, col_out, col_in,
    local, y_send, y_recv, s_send, s_recv, c_send, c_recv,
):
    rows, feats, cells = x_ref.shape
    slots = sup_ref.shape[1]
    grp = lax.axis_index("grp")
    me = lax.axis_index("src")
    shard = lax.axis_index("tgt")

    barrier = pltpu.get_barrier_semaphore()
    for step in range(1, n_src):
        pl.semaphore_signal(
            barrier, inc=1, device_id=(grp, partner(me, step, n_src), shard), device_id_type=MESH
        )
    for step in range(1, n_tgt):
        pl.semaphore_signal(
            barrier, inc=1, device_id=(grp, me, (shard + step) % n_tgt), device_id_type=MESH
        )
    fetches = [
        pltpu.make_async_copy(here, there, local.at[index])
        for index, (here, there) in enumerate(
            (
                (x_hbm, x_ref),
                (sup_hbm, sup_ref),
                (cnt_hbm, cnt_ref),
                (lms_hbm, lms_ref),
                (y_hbm, y_all.at[pl.ds(me, 1)]),
                (lmt_hbm, lm_all.at[pl.ds(me, 1)]),
                (pt_hbm, pt_all.at[pl.ds(me, 1)]),
            )
        )
    ]
    for fetch in fetches:
        fetch.start()
    pl.semaphore_wait(barrier, n_src - 1 + n_tgt - 1)

    parts = ((y_hbm, y_all), (lmt_hbm, lm_all), (pt_hbm, pt_all))

    def target_copy(index, where, step, peer):
        mine, everyone = parts[index]
        return pltpu.make_async_remote_copy(
            src_ref=mine,
            dst_ref=everyone.at[pl.ds(where, 1)],
            send_sem=y_send.at[index, step],
            recv_sem=y_recv.at[index, where],
            device_id=(grp, peer, shard),
            device_id_type=MESH,
        )

    for step in range(1, n_src):
        peer = partner(me, step, n_src)
        for index in range(3):
            target_copy(index, me, step, peer).start()
    for fetch in fetches:
        fetch.wait()

    def prepare(row, carry):
        x = x_ref[row]
        x_sq[pl.ds(row, 1)] = jnp.sum(x * x, axis=0, keepdims=True)
        high, mid, low = split3(x * (4.0 * LOG2E))
        first = jnp.concatenate([high, mid], axis=0).T.astype(jnp.bfloat16)
        second = jnp.concatenate([low, high], axis=0).T.astype(jnp.bfloat16)
        here = pl.ds(row * cells, cells)
        xt[here, 0 : 2 * feats] = first
        xt[here, 2 * feats : 4 * feats] = first
        xt[here, 4 * feats : 6 * feats] = second
        return carry

    lax.fori_loop(0, rows, prepare, 0)
    run_max[...] = jnp.full(run_max.shape, 4.0 * very_low, jnp.float32)

    limits = cnt_ref[...]
    names = lax.broadcasted_iota(jnp.int32, (n_src, rows), 0)
    joined = jnp.zeros((n_src, rows), jnp.bool_)
    for slot in range(slots):
        joined = joined | ((sup_ref[0, slot : slot + 1] == names) & (limits > slot))
    square[...] = jnp.zeros_like(square)
    square[0:n_src, 0:rows] = jnp.where(joined, 0.0, very_low)
    used[...] = square[...].T[:rows]
    row_lanes = lax.broadcasted_iota(jnp.int32, (rows, cells), 1)

    def operand(block):
        y = y_all[block]
        high, mid, low = split3(y)
        weights = jnp.concatenate([high, high, mid, mid, high, low], axis=0).astype(jnp.bfloat16)
        y_sq = jnp.sum(y * y, axis=0, keepdims=True)
        level = LOG2E * (
            lm_all[pl.ds(block, 1)] + 2.0 * pt_all[pl.ds(block, 1)] - 2.0 * y_sq
        )
        closed = jnp.sum(jnp.where(row_lanes == block, used[...], 0.0), axis=1, keepdims=True)
        return weights, level + closed

    def block_scores(blocks):
        pairs = [operand(block) for block in blocks]
        weights = jnp.concatenate([pair[0] for pair in pairs], axis=1)
        for start in range(0, rows, group):
            here = slice(start * cells, (start + group) * cells)
            cross = jnp.dot(xt[here, :], weights, preferred_element_type=jnp.float32)
            for row in range(group):
                tile = slice((start + row) * cells, (start + row + 1) * cells)
                best = run_max[tile]
                for place, block in enumerate(blocks):
                    value = (
                        cross[row * cells : (row + 1) * cells, place * cells : (place + 1) * cells]
                        + pairs[place][1][start + row : start + row + 1]
                    )
                    scores[block, tile] = value
                    best = jnp.maximum(best, value)
                run_max[tile] = best

    def await_block(step):
        block = origin(me, step, n_src)
        for index in range(3):
            target_copy(index, block, step, block).wait_recv()
        return block

    block_scores((me, await_block(1)))

    def arrival(index, carry):
        block_scores((await_block(2 * index), await_block(2 * index + 1)))
        return carry

    lax.fori_loop(1, n_src // 2, arrival, 0)

    lanes = lax.broadcasted_iota(jnp.int32, (cells, cells), 1)
    stat_col[...] = jnp.zeros_like(stat_col)

    def row_block(row):
        here = pl.ds(row * cells, cells)
        peak = jnp.max(run_max[here], axis=1, keepdims=True)
        gathered = jnp.exp2(scores[0, here] - peak)
        for block in range(1, n_src):
            gathered = gathered + jnp.exp2(scores[block, here] - peak)
        total = jnp.sum(gathered, axis=1, keepdims=True)
        return peak, total

    def row_group(index, carry):
        filled = stat_col[...]
        for place in range(group):
            row = index * group + place
            peak, total = row_block(row)
            filled = jnp.where(lanes == row, peak, filled)
            filled = jnp.where(lanes == rows + row, total, filled)
        stat_col[...] = filled
        return carry

    lax.fori_loop(0, rows // group, row_group, 0)
    stats = stat_col[...].T[: 2 * rows]
    own_peak, own_total = stats[:rows], stats[rows:]
    stat_out[...] = stats

    def stat_copy(where, step, peer):
        return pltpu.make_async_remote_copy(
            src_ref=stat_out,
            dst_ref=stat_in.at[where],
            send_sem=s_send.at[step],
            recv_sem=s_recv.at[where],
            device_id=(grp, me, peer),
            device_id_type=MESH,
        )

    for step in range(1, n_tgt):
        stat_copy(step, step, (shard + step) % n_tgt).start()
    for step in range(1, n_src):
        for index in range(3):
            target_copy(index, me, step, partner(me, step, n_src)).wait_send()
    for step in range(1, n_tgt):
        stat_copy(step, step, (shard + step) % n_tgt).wait_recv()
    peak, total = own_peak, own_total
    for step in range(1, n_tgt):
        other_peak, other_total = stat_in[step, 0:rows], stat_in[step, rows : 2 * rows]
        highest = jnp.maximum(peak, other_peak)
        total = total * jnp.exp2(peak - highest) + other_total * jnp.exp2(other_peak - highest)
        peak = highest
    joint = peak + jnp.log(total) * LOG2E
    ps_ref[...] = x_sq[...] - (entropic * LN2) * joint
    offset = LOG2E * lms_ref[...] - joint
    offset = jnp.concatenate([offset, jnp.zeros((cells - rows, cells), jnp.float32)], axis=0).T
    for row in range(rows):
        shift[row * cells : (row + 1) * cells] = jnp.broadcast_to(
            offset[:, row : row + 1], (cells, cells)
        )

    def column(block):
        many = 2 * group
        pieces = many * cells // 8

        def highest(index, best):
            here = pl.ds(index * many * cells, many * cells)
            value = scores[block, here] + shift[here]
            scores[block, here] = value
            return jnp.maximum(best, jnp.max(value.reshape(pieces, 8, cells), axis=0))

        best = jnp.full((8, cells), 4.0 * very_low, jnp.float32)
        best = lax.fori_loop(0, rows // many, highest, best)
        best = jnp.max(best, axis=0, keepdims=True)

        def add(index, summed):
            here = pl.ds(index * many * cells, many * cells)
            value = jnp.exp2(scores[block, here] - best)
            return summed + jnp.sum(value.reshape(pieces, 8, cells), axis=0)

        summed = lax.fori_loop(0, rows // many, add, jnp.zeros((8, cells), jnp.float32))
        return best, jnp.sum(summed, axis=0, keepdims=True)

    def column_copy(dest, where, step):
        return pltpu.make_async_remote_copy(
            src_ref=col_out.at[dest],
            dst_ref=col_in.at[where],
            send_sem=c_send.at[step],
            recv_sem=c_recv.at[where],
            device_id=(grp, dest, shard),
            device_id_type=MESH,
        )

    def send_column(index, carry):
        step = n_src - 1 - index
        block = partner(me, step, n_src)
        best, summed = column(block)
        col_out[block, 0:1] = best
        col_out[block, 1:2] = summed
        column_copy(block, me, step).start()
        return carry

    lax.fori_loop(0, n_src - 1, send_column, 0)
    best, summed = column(me)
    col_in[me, 0:1] = best
    col_in[me, 1:2] = summed
    for step in range(1, n_src):
        sender = origin(me, step, n_src)
        column_copy(sender, sender, step).wait_recv()
    peaks = col_in[:, 0, :]
    totals = col_in[:, 1, :]
    highest = jnp.max(peaks, axis=0, keepdims=True)
    whole = jnp.sum(totals * jnp.exp2(peaks - highest), axis=0, keepdims=True)
    pn_ref[...] = (
        pt_all[pl.ds(me, 1)]
        + entropic * lm_all[pl.ds(me, 1)]
        - (entropic * LN2) * (highest + jnp.log(whole) * LOG2E)
    )
    for step in range(1, n_tgt):
        stat_copy(step, step, (shard + step) % n_tgt).wait_send()
    for step in range(1, n_src):
        column_copy(partner(me, step, n_src), me, step).wait_send()


def dense_path(source_feat, target_feat, log_mass_src, log_mass_tgt, potential_tgt, support, counts):
    n_src, n_tgt = lax.axis_size("src"), lax.axis_size("tgt")
    rows, feats, cells = source_feat.shape
    vmem = pl.BlockSpec(memory_space=pltpu.VMEM)
    f32 = jnp.float32
    dma = pltpu.SemaphoreType.DMA
    lists = jnp.transpose(support, (1, 2, 0))
    limits = counts.T
    return pl.pallas_call(
        functools.partial(sinkhorn_kernel, n_src, n_tgt, 4),
        out_shape=(
            jax.ShapeDtypeStruct((rows, cells), f32),
            jax.ShapeDtypeStruct((1, cells), f32),
        ),
        in_specs=[pl.BlockSpec(memory_space=pl.ANY)] * 7,
        out_specs=(vmem, vmem),
        scratch_shapes=[
            pltpu.VMEM(source_feat.shape, f32),
            pltpu.VMEM((rows, cells), f32),
            pltpu.VMEM(lists.shape, jnp.int32),
            pltpu.VMEM(limits.shape, jnp.int32),
            pltpu.VMEM((n_src, feats, cells), f32),
            pltpu.VMEM((n_src, cells), f32),
            pltpu.VMEM((n_src, cells), f32),
            pltpu.VMEM((rows * cells, 6 * feats), jnp.bfloat16),
            pltpu.VMEM((n_src, rows * cells, cells), f32),
            pltpu.VMEM((rows * cells, cells), f32),
            pltpu.VMEM((cells, cells), f32),
            pltpu.VMEM((rows, cells), f32),
            pltpu.VMEM((cells, cells), f32),
            pltpu.VMEM((rows * cells, cells), f32),
            pltpu.VMEM((rows, cells), f32),
            pltpu.VMEM((2 * rows, cells), f32),
            pltpu.VMEM((n_tgt, 2 * rows, cells), f32),
            pltpu.VMEM((n_src, 2, cells), f32),
            pltpu.VMEM((n_src, 2, cells), f32),
            dma((7,)),
            dma((3, n_src)),
            dma((3, n_src)),
            dma((n_tgt,)),
            dma((n_tgt,)),
            dma((n_src,)),
            dma((n_src,)),
        ],
        compiler_params=pltpu.CompilerParams(
            collective_id=0, has_side_effects=True, vmem_limit_bytes=60 * 1024 * 1024
        ),
        name="sinkhorn",
    )(source_feat, target_feat, log_mass_src, log_mass_tgt, potential_tgt, lists, limits)


def per_device(
    source_feat, target_feat, log_mass_src, log_mass_tgt, potential_tgt, support, counts
):
    rows, feats, cells = source_feat.shape
    n_src = lax.axis_size("src")
    dense = 4 * n_src * rows * cells * cells
    fits = (
        dense <= DENSE_BYTES
        and target_feat.shape[0] == 1
        and cells % 128 == 0
        and 2 * rows <= cells
        and 2 * feats == cells
        and n_src % 8 == 0
        and rows % 8 == 0
    )
    path = dense_path if fits else general_path
    return path(
        source_feat, target_feat, log_mass_src, log_mass_tgt, potential_tgt, support, counts
    )


def solution(mesh):
    in_specs = (
        P(("grp", "src"), None, None),
        P(("grp", "src", "tgt"), None, None),
        P(("grp", "src"), None),
        P(("grp", "src", "tgt"), None),
        P(("grp", "src", "tgt"), None),
        P(("grp", "src"), "tgt", None),
        P(("grp", "src"), "tgt"),
    )
    out_specs = (P(("grp", "src"), None), P(("grp", "src", "tgt"), None))
    return jax.shard_map(
        per_device, mesh=mesh, in_specs=in_specs, out_specs=out_specs, check_vma=False
    )
```

```python
import functools
import math

import jax
import jax.numpy as jnp
from jax import lax
from jax.experimental import pallas as pl
from jax.experimental.pallas import tpu as pltpu
from jax.sharding import PartitionSpec as P

entropic = 0.5
very_low = -1e30


def merged(part, axis, combine):
    gathered = jax.tree.map(lambda a: lax.all_gather(a, axis), part)

    def take(source):
        return jax.tree.map(lambda a: lax.dynamic_index_in_dim(a, source, 0, False), gathered)

    return lax.fori_loop(
        1, lax.axis_size(axis), lambda source, state: combine(state, take(source)), take(0)
    )


def cost_tiles(source_blk, source_sq, target_blk, target_sq):
    cross = jnp.einsum(
        "...fi,...fj->...ij", source_blk, target_blk, precision=lax.Precision.HIGHEST
    )
    return source_sq[..., :, None] + target_sq[..., None, :] - 2.0 * cross


def row_stats(cost, mass_tgt, poten_tgt, usable):
    scores = mass_tgt[..., None, :] + (poten_tgt[..., None, :] - cost) / entropic
    scores = jnp.where(usable[..., None, None], scores, very_low)
    peak = jnp.max(scores, axis=(1, 3))
    total = jnp.sum(jnp.exp(scores - peak[:, None, :, None]), axis=(1, 3))
    return (peak, total)


def column_stats(cost, mass_src, poten_src, usable):
    scores = mass_src[:, None, :, None] + (poten_src[:, None, :, None] - cost) / entropic
    peak = jnp.max(scores, axis=2)
    total = jnp.sum(jnp.exp(scores - peak[:, :, None, :]), axis=2)
    peak = jnp.where(usable[..., None], peak, very_low)
    total = jnp.where(usable[..., None], total, 0.0)
    return (peak, total)


def merge_pair(first_pair, second_pair):
    first_peak, first_total = first_pair
    second_peak, second_total = second_pair
    highest = jnp.maximum(first_peak, second_peak)
    summed = first_total * jnp.exp(first_peak - highest) + second_total * jnp.exp(
        second_peak - highest
    )
    return (highest, summed)


def segment_merge(peaks, totals, seg_ids, segments):
    best = jax.ops.segment_max(peaks, seg_ids, num_segments=segments + 1)
    best = jnp.maximum(best, very_low)
    summed = jax.ops.segment_sum(
        totals * jnp.exp(peaks - best[seg_ids]), seg_ids, num_segments=segments + 1
    )
    return (best[:segments], summed[:segments])


def general_path(
    source_feat, target_feat, log_mass_src, log_mass_tgt, potential_tgt, support, counts
):
    target_all, mass_all, poten_all = (
        lax.all_gather(target_feat, "src", axis=0, tiled=True),
        lax.all_gather(log_mass_tgt, "src", axis=0, tiled=True),
        lax.all_gather(potential_tgt, "src", axis=0, tiled=True),
    )
    blocks = target_all.shape[0]
    rows_here = source_feat.shape[0]
    slots_here = support.shape[2]
    cells = source_feat.shape[2]
    indices = support[:, 0, :]
    limits = counts[:, 0]
    usable = jnp.arange(slots_here, dtype=jnp.int32)[None, :] < limits[:, None]
    source_sq = jnp.sum(source_feat * source_feat, axis=1)
    target_sq = jnp.sum(target_all * target_all, axis=1)
    width = math.gcd(rows_here, 4)

    def grouped(array):
        return array.reshape((rows_here // width, width) + array.shape[1:])

    def row_pass(items):
        source_blk, source_nrm, ids_here, use_here = items
        cost = cost_tiles(
            source_blk[:, None], source_nrm[:, None], target_all[ids_here], target_sq[ids_here]
        )
        return row_stats(cost, mass_all[ids_here], poten_all[ids_here], use_here)

    peak, total = lax.map(
        row_pass, (grouped(source_feat), grouped(source_sq), grouped(indices), grouped(usable))
    )
    peak = peak.reshape(rows_here, cells)
    total = total.reshape(rows_here, cells)
    peak_all, total_all = merged((peak, total), "tgt", merge_pair)
    potential_src = -entropic * (peak_all + jnp.log(total_all))

    def column_pass(items):
        source_blk, source_nrm, mass_here, poten_here, ids_here, use_here = items
        cost = cost_tiles(
            source_blk[:, None], source_nrm[:, None], target_all[ids_here], target_sq[ids_here]
        )
        return column_stats(cost, mass_here, poten_here, use_here)

    peaks, totals = lax.map(
        column_pass,
        (
            grouped(source_feat),
            grouped(source_sq),
            grouped(log_mass_src),
            grouped(potential_src),
            grouped(indices),
            grouped(usable),
        ),
    )
    seg_ids = jnp.where(usable, indices, blocks).reshape(-1)
    best, summed = segment_merge(
        peaks.reshape(-1, cells), totals.reshape(-1, cells), seg_ids, blocks
    )
    share = blocks // lax.axis_size("src")
    own_start = lax.axis_index("src") * share
    highest = lax.pmax(best, "src")
    whole = lax.psum(summed * jnp.exp(best - highest), "src")
    own_peak = lax.dynamic_slice_in_dim(highest, own_start, share, 0)
    own_total = lax.dynamic_slice_in_dim(whole, own_start, share, 0)
    potential_new = -entropic * (own_peak + jnp.log(own_total))
    return (potential_src, potential_new)


LOG2E = 1.4426950408889634
LN2 = 0.6931471805599453
MESH = pl.DeviceIdType.MESH
DENSE_BYTES = 24 * 1024 * 1024


def split3(value):
    high = value.astype(jnp.bfloat16).astype(jnp.float32)
    rest = value - high
    mid = rest.astype(jnp.bfloat16).astype(jnp.float32)
    return high, mid, rest - mid


def partner(me, step, count):
    if count & (count - 1):
        return (me + step) % count
    met, bit = 0, 1
    while bit < count:
        met = met + bit * ((me // bit + step // bit) % 2)
        bit *= 2
    return met


def origin(me, step, count):
    if count & (count - 1):
        return (me - step + count) % count
    return partner(me, step, count)


def sinkhorn_kernel(
    n_src, n_tgt, group,
    x_hbm, y_hbm, lms_hbm, lmt_hbm, pt_hbm, sup_hbm, cnt_hbm,
    ps_ref, pn_ref,
    x_ref, lms_ref, sup_ref, cnt_ref,
    y_all, lm_all, pt_all, xt, scores, square, used, stat_col, shift,
    x_sq, stat_out, stat_in, col_out, col_in,
    local, y_send, y_recv, s_send, s_recv, c_send, c_recv,
):
    rows, feats, cells = x_ref.shape
    slots = sup_ref.shape[1]
    grp = lax.axis_index("grp")
    me = lax.axis_index("src")
    shard = lax.axis_index("tgt")

    barrier = pltpu.get_barrier_semaphore()
    for step in range(1, n_src):
        pl.semaphore_signal(
            barrier, inc=1, device_id=(grp, partner(me, step, n_src), shard), device_id_type=MESH
        )
    for step in range(1, n_tgt):
        pl.semaphore_signal(
            barrier, inc=1, device_id=(grp, me, (shard + step) % n_tgt), device_id_type=MESH
        )
    fetches = [
        pltpu.make_async_copy(here, there, local.at[index])
        for index, (here, there) in enumerate(
            (
                (x_hbm, x_ref),
                (sup_hbm, sup_ref),
                (cnt_hbm, cnt_ref),
                (lms_hbm, lms_ref),
                (y_hbm, y_all.at[pl.ds(me, 1)]),
                (lmt_hbm, lm_all.at[pl.ds(me, 1)]),
                (pt_hbm, pt_all.at[pl.ds(me, 1)]),
            )
        )
    ]
    for fetch in fetches:
        fetch.start()
    pl.semaphore_wait(barrier, n_src - 1 + n_tgt - 1)

    parts = ((y_hbm, y_all), (lmt_hbm, lm_all), (pt_hbm, pt_all))

    def target_copy(index, where, step, peer):
        mine, everyone = parts[index]
        return pltpu.make_async_remote_copy(
            src_ref=mine,
            dst_ref=everyone.at[pl.ds(where, 1)],
            send_sem=y_send.at[index, step],
            recv_sem=y_recv.at[index, where],
            device_id=(grp, peer, shard),
            device_id_type=MESH,
        )

    for step in range(1, n_src):
        peer = partner(me, step, n_src)
        for index in range(3):
            target_copy(index, me, step, peer).start()
    for fetch in fetches:
        fetch.wait()

    def prepare(row, carry):
        x = x_ref[row]
        x_sq[pl.ds(row, 1)] = jnp.sum(x * x, axis=0, keepdims=True)
        high, mid, low = split3(x * (4.0 * LOG2E))
        first = jnp.concatenate([high, mid], axis=0).T.astype(jnp.bfloat16)
        second = jnp.concatenate([low, high], axis=0).T.astype(jnp.bfloat16)
        here = pl.ds(row * cells, cells)
        xt[here, 0 : 2 * feats] = first
        xt[here, 2 * feats : 4 * feats] = first
        xt[here, 4 * feats : 6 * feats] = second
        return carry

    lax.fori_loop(0, rows, prepare, 0)

    limits = cnt_ref[...]
    names = lax.broadcasted_iota(jnp.int32, (n_src, rows), 0)
    joined = jnp.zeros((n_src, rows), jnp.bool_)
    for slot in range(slots):
        joined = joined | ((sup_ref[0, slot : slot + 1] == names) & (limits > slot))
    square[...] = jnp.zeros_like(square)
    square[0:n_src, 0:rows] = jnp.where(joined, 0.0, very_low)
    used[...] = square[...].T[:rows]
    row_lanes = lax.broadcasted_iota(jnp.int32, (rows, cells), 1)

    def operand(block):
        y = y_all[block]
        high, mid, low = split3(y)
        weights = jnp.concatenate([high, high, mid, mid, high, low], axis=0).astype(jnp.bfloat16)
        y_sq = jnp.sum(y * y, axis=0, keepdims=True)
        level = LOG2E * (
            lm_all[pl.ds(block, 1)] + 2.0 * pt_all[pl.ds(block, 1)] - 2.0 * y_sq
        )
        closed = jnp.sum(jnp.where(row_lanes == block, used[...], 0.0), axis=1, keepdims=True)
        return weights, level + closed

    lanes = lax.broadcasted_iota(jnp.int32, (cells, cells), 1)
    stat_col[...] = jnp.zeros_like(stat_col)

    def block_scores(turn, blocks):
        pairs = [operand(block) for block in blocks]
        weights = jnp.concatenate([pair[0] for pair in pairs], axis=1)
        filled = stat_col[...]
        for start in range(0, rows, group):
            here = slice(start * cells, (start + group) * cells)
            cross = jnp.dot(xt[here, :], weights, preferred_element_type=jnp.float32)
            for part in range(group):
                row = start + part
                tile = slice(row * cells, (row + 1) * cells)
                values = [
                    cross[part * cells : (part + 1) * cells, place * cells : (place + 1) * cells]
                    + pairs[place][1][row : row + 1]
                    for place in range(len(blocks))
                ]
                for block, value in zip(blocks, values):
                    scores[block, tile] = value
                peak = jnp.max(functools.reduce(jnp.maximum, values), axis=1, keepdims=True)
                total = functools.reduce(jnp.add, [jnp.exp2(value - peak) for value in values])
                total = jnp.sum(total, axis=1, keepdims=True)
                lane = turn * (2 * rows) + row
                filled = jnp.where(lanes == lane, peak, filled)
                filled = jnp.where(lanes == lane + rows, total, filled)
        stat_col[...] = filled

    def await_block(step):
        block = origin(me, step, n_src)
        for index in range(3):
            target_copy(index, block, step, block).wait_recv()
        return block

    block_scores(0, (me, await_block(1)))

    def arrival(index, carry):
        block_scores(index, (await_block(2 * index), await_block(2 * index + 1)))
        return carry

    lax.fori_loop(1, n_src // 2, arrival, 0)

    def joined_stats(first, second):
        highest = jnp.maximum(first[0], second[0])
        summed = first[1] * jnp.exp2(first[0] - highest) + second[1] * jnp.exp2(second[0] - highest)
        return highest, summed

    stats = stat_col[...].T
    turns = [
        (stats[2 * rows * turn :][:rows], stats[2 * rows * turn + rows :][:rows])
        for turn in range(n_src // 2)
    ]
    while len(turns) > 1:
        turns = [joined_stats(*turns[place : place + 2]) for place in range(0, len(turns), 2)]
    own_peak, own_total = turns[0]
    stat_out[0:rows] = own_peak
    stat_out[rows : 2 * rows] = own_total

    def stat_copy(where, step, peer):
        return pltpu.make_async_remote_copy(
            src_ref=stat_out,
            dst_ref=stat_in.at[where],
            send_sem=s_send.at[step],
            recv_sem=s_recv.at[where],
            device_id=(grp, me, peer),
            device_id_type=MESH,
        )

    for step in range(1, n_tgt):
        stat_copy(step, step, (shard + step) % n_tgt).start()
    for step in range(1, n_src):
        for index in range(3):
            target_copy(index, me, step, partner(me, step, n_src)).wait_send()
    for step in range(1, n_tgt):
        stat_copy(step, step, (shard + step) % n_tgt).wait_recv()
    peak, total = own_peak, own_total
    for step in range(1, n_tgt):
        other = (stat_in[step, 0:rows], stat_in[step, rows : 2 * rows])
        peak, total = joined_stats((peak, total), other)
    joint = peak + jnp.log(total) * LOG2E
    ps_ref[...] = x_sq[...] - (entropic * LN2) * joint
    offset = LOG2E * lms_ref[...] - joint
    offset = jnp.concatenate([offset, jnp.zeros((cells - rows, cells), jnp.float32)], axis=0).T
    for row in range(rows):
        shift[row * cells : (row + 1) * cells] = jnp.broadcast_to(
            offset[:, row : row + 1], (cells, cells)
        )

    many = 2 * group
    pieces = many * cells // 8
    lowest = jnp.full((8, cells), 4.0 * very_low, jnp.float32)
    nothing = jnp.zeros((8, cells), jnp.float32)

    def find(block, here, best):
        value = scores[block, here] + shift[here]
        return jnp.maximum(best, jnp.max(value.reshape(pieces, 8, cells), axis=0))

    def add(block, here, best, summed):
        value = jnp.exp2(scores[block, here] + shift[here] - best)
        return summed + jnp.sum(value.reshape(pieces, 8, cells), axis=0)

    def span(index):
        return pl.ds(index * many * cells, many * cells)

    def whole_column(summed):
        return jnp.sum(summed, axis=0, keepdims=True)

    def peak_of(best):
        return jnp.max(best, axis=0, keepdims=True)

    def column_copy(dest, where, step):
        return pltpu.make_async_remote_copy(
            src_ref=col_out.at[dest],
            dst_ref=col_in.at[where],
            send_sem=c_send.at[step],
            recv_sem=c_recv.at[where],
            device_id=(grp, dest, shard),
            device_id_type=MESH,
        )

    def send_column(index, best):
        step = n_src - 1 - index
        block = partner(me, step, n_src)
        following = partner(me, step - 1, n_src)
        summed, later = nothing, lowest
        for part in range(rows // many):
            summed = add(block, span(part), best, summed)
            later = find(following, span(part), later)
        col_out[block, 0:1] = best
        col_out[block, 1:2] = whole_column(summed)
        column_copy(block, me, step).start()
        return peak_of(later)

    farthest = partner(me, n_src - 1, n_src)
    best = lowest
    for part in range(rows // many):
        best = find(farthest, span(part), best)
    best = lax.fori_loop(0, n_src - 1, send_column, peak_of(best))
    summed = nothing
    for part in range(rows // many):
        summed = add(me, span(part), best, summed)
    summed = whole_column(summed)
    col_in[me, 0:1] = best
    col_in[me, 1:2] = summed
    for step in range(1, n_src):
        sender = origin(me, step, n_src)
        column_copy(sender, sender, step).wait_recv()
    peaks = col_in[:, 0, :]
    totals = col_in[:, 1, :]
    highest = jnp.max(peaks, axis=0, keepdims=True)
    whole = jnp.sum(totals * jnp.exp2(peaks - highest), axis=0, keepdims=True)
    pn_ref[...] = (
        pt_all[pl.ds(me, 1)]
        + entropic * lm_all[pl.ds(me, 1)]
        - (entropic * LN2) * (highest + jnp.log(whole) * LOG2E)
    )
    for step in range(1, n_tgt):
        stat_copy(step, step, (shard + step) % n_tgt).wait_send()
    for step in range(1, n_src):
        column_copy(partner(me, step, n_src), me, step).wait_send()


def dense_path(source_feat, target_feat, log_mass_src, log_mass_tgt, potential_tgt, support, counts):
    n_src, n_tgt = lax.axis_size("src"), lax.axis_size("tgt")
    rows, feats, cells = source_feat.shape
    vmem = pl.BlockSpec(memory_space=pltpu.VMEM)
    f32 = jnp.float32
    dma = pltpu.SemaphoreType.DMA
    lists = jnp.transpose(support, (1, 2, 0))
    limits = counts.T
    return pl.pallas_call(
        functools.partial(sinkhorn_kernel, n_src, n_tgt, 4),
        out_shape=(
            jax.ShapeDtypeStruct((rows, cells), f32),
            jax.ShapeDtypeStruct((1, cells), f32),
        ),
        in_specs=[pl.BlockSpec(memory_space=pl.ANY)] * 7,
        out_specs=(vmem, vmem),
        scratch_shapes=[
            pltpu.VMEM(source_feat.shape, f32),
            pltpu.VMEM((rows, cells), f32),
            pltpu.VMEM(lists.shape, jnp.int32),
            pltpu.VMEM(limits.shape, jnp.int32),
            pltpu.VMEM((n_src, feats, cells), f32),
            pltpu.VMEM((n_src, cells), f32),
            pltpu.VMEM((n_src, cells), f32),
            pltpu.VMEM((rows * cells, 6 * feats), jnp.bfloat16),
            pltpu.VMEM((n_src, rows * cells, cells), f32),
            pltpu.VMEM((cells, cells), f32),
            pltpu.VMEM((rows, cells), f32),
            pltpu.VMEM((cells, cells), f32),
            pltpu.VMEM((rows * cells, cells), f32),
            pltpu.VMEM((rows, cells), f32),
            pltpu.VMEM((2 * rows, cells), f32),
            pltpu.VMEM((n_tgt, 2 * rows, cells), f32),
            pltpu.VMEM((n_src, 2, cells), f32),
            pltpu.VMEM((n_src, 2, cells), f32),
            dma((7,)),
            dma((3, n_src)),
            dma((3, n_src)),
            dma((n_tgt,)),
            dma((n_tgt,)),
            dma((n_src,)),
            dma((n_src,)),
        ],
        compiler_params=pltpu.CompilerParams(
            collective_id=0, has_side_effects=True, vmem_limit_bytes=60 * 1024 * 1024
        ),
        name="sinkhorn",
    )(source_feat, target_feat, log_mass_src, log_mass_tgt, potential_tgt, lists, limits)


def per_device(
    source_feat, target_feat, log_mass_src, log_mass_tgt, potential_tgt, support, counts
):
    rows, feats, cells = source_feat.shape
    n_src = lax.axis_size("src")
    dense = 4 * n_src * rows * cells * cells
    fits = (
        dense <= DENSE_BYTES
        and target_feat.shape[0] == 1
        and cells % 128 == 0
        and n_src * rows <= cells
        and rows % 8 == 0
        and not (n_src // 2) & (n_src // 2 - 1)
        and 2 * feats == cells
        and n_src % 8 == 0
        and rows % 8 == 0
    )
    path = dense_path if fits else general_path
    return path(
        source_feat, target_feat, log_mass_src, log_mass_tgt, potential_tgt, support, counts
    )


def solution(mesh):
    in_specs = (
        P(("grp", "src"), None, None),
        P(("grp", "src", "tgt"), None, None),
        P(("grp", "src"), None),
        P(("grp", "src", "tgt"), None),
        P(("grp", "src", "tgt"), None),
        P(("grp", "src"), "tgt", None),
        P(("grp", "src"), "tgt"),
    )
    out_specs = (P(("grp", "src"), None), P(("grp", "src", "tgt"), None))
    return jax.shard_map(
        per_device, mesh=mesh, in_specs=in_specs, out_specs=out_specs, check_vma=False
    )
```

```python
import functools
import math

import jax
import jax.numpy as jnp
from jax import lax
from jax.experimental import pallas as pl
from jax.experimental.pallas import tpu as pltpu
from jax.sharding import PartitionSpec as P

entropic = 0.5
very_low = -1e30


def merged(part, axis, combine):
    gathered = jax.tree.map(lambda a: lax.all_gather(a, axis), part)

    def take(source):
        return jax.tree.map(lambda a: lax.dynamic_index_in_dim(a, source, 0, False), gathered)

    return lax.fori_loop(
        1, lax.axis_size(axis), lambda source, state: combine(state, take(source)), take(0)
    )


def cost_tiles(source_blk, source_sq, target_blk, target_sq):
    cross = jnp.einsum(
        "...fi,...fj->...ij", source_blk, target_blk, precision=lax.Precision.HIGHEST
    )
    return source_sq[..., :, None] + target_sq[..., None, :] - 2.0 * cross


def row_stats(cost, mass_tgt, poten_tgt, usable):
    scores = mass_tgt[..., None, :] + (poten_tgt[..., None, :] - cost) / entropic
    scores = jnp.where(usable[..., None, None], scores, very_low)
    peak = jnp.max(scores, axis=(1, 3))
    total = jnp.sum(jnp.exp(scores - peak[:, None, :, None]), axis=(1, 3))
    return (peak, total)


def column_stats(cost, mass_src, poten_src, usable):
    scores = mass_src[:, None, :, None] + (poten_src[:, None, :, None] - cost) / entropic
    peak = jnp.max(scores, axis=2)
    total = jnp.sum(jnp.exp(scores - peak[:, :, None, :]), axis=2)
    peak = jnp.where(usable[..., None], peak, very_low)
    total = jnp.where(usable[..., None], total, 0.0)
    return (peak, total)


def merge_pair(first_pair, second_pair):
    first_peak, first_total = first_pair
    second_peak, second_total = second_pair
    highest = jnp.maximum(first_peak, second_peak)
    summed = first_total * jnp.exp(first_peak - highest) + second_total * jnp.exp(
        second_peak - highest
    )
    return (highest, summed)


def segment_merge(peaks, totals, seg_ids, segments):
    best = jax.ops.segment_max(peaks, seg_ids, num_segments=segments + 1)
    best = jnp.maximum(best, very_low)
    summed = jax.ops.segment_sum(
        totals * jnp.exp(peaks - best[seg_ids]), seg_ids, num_segments=segments + 1
    )
    return (best[:segments], summed[:segments])


def general_path(
    source_feat, target_feat, log_mass_src, log_mass_tgt, potential_tgt, support, counts
):
    target_all, mass_all, poten_all = (
        lax.all_gather(target_feat, "src", axis=0, tiled=True),
        lax.all_gather(log_mass_tgt, "src", axis=0, tiled=True),
        lax.all_gather(potential_tgt, "src", axis=0, tiled=True),
    )
    blocks = target_all.shape[0]
    rows_here = source_feat.shape[0]
    slots_here = support.shape[2]
    cells = source_feat.shape[2]
    indices = support[:, 0, :]
    limits = counts[:, 0]
    usable = jnp.arange(slots_here, dtype=jnp.int32)[None, :] < limits[:, None]
    source_sq = jnp.sum(source_feat * source_feat, axis=1)
    target_sq = jnp.sum(target_all * target_all, axis=1)
    width = math.gcd(rows_here, 4)

    def grouped(array):
        return array.reshape((rows_here // width, width) + array.shape[1:])

    def row_pass(items):
        source_blk, source_nrm, ids_here, use_here = items
        cost = cost_tiles(
            source_blk[:, None], source_nrm[:, None], target_all[ids_here], target_sq[ids_here]
        )
        return row_stats(cost, mass_all[ids_here], poten_all[ids_here], use_here)

    peak, total = lax.map(
        row_pass, (grouped(source_feat), grouped(source_sq), grouped(indices), grouped(usable))
    )
    peak = peak.reshape(rows_here, cells)
    total = total.reshape(rows_here, cells)
    peak_all, total_all = merged((peak, total), "tgt", merge_pair)
    potential_src = -entropic * (peak_all + jnp.log(total_all))

    def column_pass(items):
        source_blk, source_nrm, mass_here, poten_here, ids_here, use_here = items
        cost = cost_tiles(
            source_blk[:, None], source_nrm[:, None], target_all[ids_here], target_sq[ids_here]
        )
        return column_stats(cost, mass_here, poten_here, use_here)

    peaks, totals = lax.map(
        column_pass,
        (
            grouped(source_feat),
            grouped(source_sq),
            grouped(log_mass_src),
            grouped(potential_src),
            grouped(indices),
            grouped(usable),
        ),
    )
    seg_ids = jnp.where(usable, indices, blocks).reshape(-1)
    best, summed = segment_merge(
        peaks.reshape(-1, cells), totals.reshape(-1, cells), seg_ids, blocks
    )
    share = blocks // lax.axis_size("src")
    own_start = lax.axis_index("src") * share
    highest = lax.pmax(best, "src")
    whole = lax.psum(summed * jnp.exp(best - highest), "src")
    own_peak = lax.dynamic_slice_in_dim(highest, own_start, share, 0)
    own_total = lax.dynamic_slice_in_dim(whole, own_start, share, 0)
    potential_new = -entropic * (own_peak + jnp.log(own_total))
    return (potential_src, potential_new)


LOG2E = 1.4426950408889634
LN2 = 0.6931471805599453
MESH = pl.DeviceIdType.MESH
DENSE_BYTES = 24 * 1024 * 1024


def split3(value):
    high = value.astype(jnp.bfloat16).astype(jnp.float32)
    rest = value - high
    mid = rest.astype(jnp.bfloat16).astype(jnp.float32)
    return high, mid, rest - mid


def partner(me, step, count):
    met, bit = 0, 1
    while bit < count:
        met = met + bit * ((me // bit + step // bit) % 2)
        bit *= 2
    return met


def sinkhorn_kernel(
    n_src, n_tgt, group,
    x_hbm, y_hbm, lms_hbm, lmt_hbm, pt_hbm, sup_hbm, cnt_hbm,
    ps_ref, pn_ref,
    x_ref, lms_ref, sup_ref, cnt_ref,
    y_all, lm_all, pt_all, xt, scores, square, used, stat_col, shift,
    x_sq, stat_out, stat_in, col_out, col_in,
    local, y_send, y_recv, s_send, s_recv, c_send, c_recv,
):
    rows, feats, cells = x_ref.shape
    slots = sup_ref.shape[1]
    grp = lax.axis_index("grp")
    me = lax.axis_index("src")
    shard = lax.axis_index("tgt")

    barrier = pltpu.get_barrier_semaphore()
    for step in range(1, n_src):
        pl.semaphore_signal(
            barrier, inc=1, device_id=(grp, partner(me, step, n_src), shard), device_id_type=MESH
        )
    for step in range(1, n_tgt):
        pl.semaphore_signal(
            barrier, inc=1, device_id=(grp, me, (shard + step) % n_tgt), device_id_type=MESH
        )
    fetches = [
        pltpu.make_async_copy(here, there, local.at[index])
        for index, (here, there) in enumerate(
            (
                (x_hbm, x_ref),
                (sup_hbm, sup_ref),
                (cnt_hbm, cnt_ref),
                (lms_hbm, lms_ref),
                (y_hbm, y_all.at[pl.ds(me, 1)]),
                (lmt_hbm, lm_all.at[pl.ds(me, 1)]),
                (pt_hbm, pt_all.at[pl.ds(me, 1)]),
            )
        )
    ]
    for fetch in fetches:
        fetch.start()
    pl.semaphore_wait(barrier, n_src - 1 + n_tgt - 1)

    parts = ((y_hbm, y_all), (lmt_hbm, lm_all), (pt_hbm, pt_all))

    def target_copy(index, where, step, peer):
        mine, everyone = parts[index]
        return pltpu.make_async_remote_copy(
            src_ref=mine,
            dst_ref=everyone.at[pl.ds(where, 1)],
            send_sem=y_send.at[index, step],
            recv_sem=y_recv.at[index, where],
            device_id=(grp, peer, shard),
            device_id_type=MESH,
        )

    def relay(step):
        block = partner(me, step, n_src)
        return pltpu.make_async_remote_copy(
            src_ref=y_all.at[pl.ds(block, 1)],
            dst_ref=y_all.at[pl.ds(block, 1)],
            send_sem=y_send.at[0, step + 1],
            recv_sem=y_recv.at[0, block],
            device_id=(grp, partner(me, 1, n_src), shard),
            device_id_type=MESH,
        )

    far_steps = range(n_src - 2, 0, -2)
    for step in (1, *far_steps):
        target_copy(0, me, step, partner(me, step, n_src)).start()
    for step in range(1, n_src):
        for index in (1, 2):
            target_copy(index, me, step, partner(me, step, n_src)).start()
    for fetch in fetches:
        fetch.wait()

    def prepare(row, carry):
        x = x_ref[row]
        x_sq[pl.ds(row, 1)] = jnp.sum(x * x, axis=0, keepdims=True)
        high, mid, low = split3(x * (4.0 * LOG2E))
        first = jnp.concatenate([high, mid], axis=0).T.astype(jnp.bfloat16)
        second = jnp.concatenate([low, high], axis=0).T.astype(jnp.bfloat16)
        here = pl.ds(row * cells, cells)
        xt[here, 0 : 2 * feats] = first
        xt[here, 2 * feats : 4 * feats] = first
        xt[here, 4 * feats : 6 * feats] = second
        return carry

    lax.fori_loop(0, rows, prepare, 0)

    limits = cnt_ref[...]
    names = lax.broadcasted_iota(jnp.int32, (n_src, rows), 0)
    joined = jnp.zeros((n_src, rows), jnp.bool_)
    for slot in range(slots):
        joined = joined | ((sup_ref[0, slot : slot + 1] == names) & (limits > slot))
    square[...] = jnp.zeros_like(square)
    square[0:n_src, 0:rows] = jnp.where(joined, 0.0, very_low)
    used[...] = square[...].T[:rows]
    row_lanes = lax.broadcasted_iota(jnp.int32, (rows, cells), 1)

    def operand(block):
        y = y_all[block]
        high, mid, low = split3(y)
        weights = jnp.concatenate([high, high, mid, mid, high, low], axis=0).astype(jnp.bfloat16)
        y_sq = jnp.sum(y * y, axis=0, keepdims=True)
        level = LOG2E * (
            lm_all[pl.ds(block, 1)] + 2.0 * pt_all[pl.ds(block, 1)] - 2.0 * y_sq
        )
        closed = jnp.sum(jnp.where(row_lanes == block, used[...], 0.0), axis=1, keepdims=True)
        return weights, level + closed

    lanes = lax.broadcasted_iota(jnp.int32, (cells, cells), 1)
    stat_col[...] = jnp.zeros_like(stat_col)

    def block_scores(turn, blocks):
        pairs = [operand(block) for block in blocks]
        weights = jnp.concatenate([pair[0] for pair in pairs], axis=1)
        filled = stat_col[...]
        for start in range(0, rows, group):
            here = slice(start * cells, (start + group) * cells)
            cross = jnp.dot(xt[here, :], weights, preferred_element_type=jnp.float32)
            for part in range(group):
                row = start + part
                tile = slice(row * cells, (row + 1) * cells)
                values = [
                    cross[part * cells : (part + 1) * cells, place * cells : (place + 1) * cells]
                    + pairs[place][1][row : row + 1]
                    for place in range(len(blocks))
                ]
                for block, value in zip(blocks, values):
                    scores[block, tile] = value
                peak = jnp.max(functools.reduce(jnp.maximum, values), axis=1, keepdims=True)
                total = functools.reduce(jnp.add, [jnp.exp2(value - peak) for value in values])
                total = jnp.sum(total, axis=1, keepdims=True)
                lane = turn * (2 * rows) + row
                filled = jnp.where(lanes == lane, peak, filled)
                filled = jnp.where(lanes == lane + rows, total, filled)
        stat_col[...] = filled

    def await_part(index, step):
        block = partner(me, step, n_src)
        target_copy(index, block, step, block).wait_recv()

    def await_pair(turn):
        for index in (1, 2):
            await_part(index, 2 * turn)
            await_part(index, 2 * turn + 1)
        await_part(0, 2 * turn + 1)
        return partner(me, 2 * turn, n_src), partner(me, 2 * turn + 1, n_src)

    for index in range(3):
        await_part(index, 1)
    block_scores(0, (me, partner(me, 1, n_src)))
    for step in reversed(far_steps):
        await_part(0, step)
        relay(step).start()

    def arrival(turn, carry):
        block_scores(turn, await_pair(turn))
        return carry

    lax.fori_loop(1, n_src // 2, arrival, 0)

    def joined_stats(first, second):
        highest = jnp.maximum(first[0], second[0])
        summed = first[1] * jnp.exp2(first[0] - highest) + second[1] * jnp.exp2(second[0] - highest)
        return highest, summed

    stats = stat_col[...].T
    turns = [
        (stats[2 * rows * turn :][:rows], stats[2 * rows * turn + rows :][:rows])
        for turn in range(n_src // 2)
    ]
    while len(turns) > 1:
        turns = [joined_stats(*turns[place : place + 2]) for place in range(0, len(turns), 2)]
    own_peak, own_total = turns[0]
    stat_out[0:rows] = own_peak
    stat_out[rows : 2 * rows] = own_total

    def stat_copy(where, step, peer):
        return pltpu.make_async_remote_copy(
            src_ref=stat_out,
            dst_ref=stat_in.at[where],
            send_sem=s_send.at[step],
            recv_sem=s_recv.at[where],
            device_id=(grp, me, peer),
            device_id_type=MESH,
        )

    for step in range(1, n_tgt):
        stat_copy(step, step, (shard + step) % n_tgt).start()
    for step in (1, *far_steps):
        target_copy(0, me, step, partner(me, step, n_src)).wait_send()
    for step in far_steps:
        relay(step).wait_send()
    for step in range(1, n_src):
        for index in (1, 2):
            target_copy(index, me, step, partner(me, step, n_src)).wait_send()
    for step in range(1, n_tgt):
        stat_copy(step, step, (shard + step) % n_tgt).wait_recv()
    peak, total = own_peak, own_total
    for step in range(1, n_tgt):
        other = (stat_in[step, 0:rows], stat_in[step, rows : 2 * rows])
        peak, total = joined_stats((peak, total), other)
    joint = peak + jnp.log(total) * LOG2E
    ps_ref[...] = x_sq[...] - (entropic * LN2) * joint
    offset = LOG2E * lms_ref[...] - joint
    offset = jnp.concatenate([offset, jnp.zeros((cells - rows, cells), jnp.float32)], axis=0).T
    for row in range(rows):
        shift[row * cells : (row + 1) * cells] = jnp.broadcast_to(
            offset[:, row : row + 1], (cells, cells)
        )

    many = 8
    pieces = many * cells // 8
    lowest = jnp.full((8, cells), 4.0 * very_low, jnp.float32)
    nothing = jnp.zeros((8, cells), jnp.float32)

    def find(block, here, best):
        value = scores[block, here] + shift[here]
        return jnp.maximum(best, jnp.max(value.reshape(pieces, 8, cells), axis=0))

    def add(block, here, best, summed):
        value = jnp.exp2(scores[block, here] + shift[here] - best)
        return summed + jnp.sum(value.reshape(pieces, 8, cells), axis=0)

    def span(index):
        return pl.ds(index * many * cells, many * cells)

    def whole_column(summed):
        return jnp.sum(summed, axis=0, keepdims=True)

    def peak_of(best):
        return jnp.max(best, axis=0, keepdims=True)

    def column_copy(dest, where, step):
        return pltpu.make_async_remote_copy(
            src_ref=col_out.at[dest],
            dst_ref=col_in.at[where],
            send_sem=c_send.at[step],
            recv_sem=c_recv.at[where],
            device_id=(grp, dest, shard),
            device_id_type=MESH,
        )

    def send_column(index, best):
        step = n_src - 1 - index
        block = partner(me, step, n_src)
        following = partner(me, step - 1, n_src)
        summed, later = nothing, lowest
        for part in range(rows // many):
            summed = add(block, span(part), best, summed)
            later = find(following, span(part), later)
        col_out[block, 0:1] = best
        col_out[block, 1:2] = whole_column(summed)
        column_copy(block, me, step).start()
        return peak_of(later)

    farthest = partner(me, n_src - 1, n_src)
    best = lowest
    for part in range(rows // many):
        best = find(farthest, span(part), best)
    best = lax.fori_loop(0, n_src - 1, send_column, peak_of(best))
    summed = nothing
    for part in range(rows // many):
        summed = add(me, span(part), best, summed)
    summed = whole_column(summed)
    col_in[me, 0:1] = best
    col_in[me, 1:2] = summed
    for step in range(1, n_src):
        sender = partner(me, step, n_src)
        column_copy(sender, sender, step).wait_recv()
    peaks = col_in[:, 0, :]
    totals = col_in[:, 1, :]
    highest = jnp.max(peaks, axis=0, keepdims=True)
    whole = jnp.sum(totals * jnp.exp2(peaks - highest), axis=0, keepdims=True)
    pn_ref[...] = (
        pt_all[pl.ds(me, 1)]
        + entropic * lm_all[pl.ds(me, 1)]
        - (entropic * LN2) * (highest + jnp.log(whole) * LOG2E)
    )
    for step in range(1, n_tgt):
        stat_copy(step, step, (shard + step) % n_tgt).wait_send()
    for step in range(1, n_src):
        column_copy(partner(me, step, n_src), me, step).wait_send()


def dense_path(source_feat, target_feat, log_mass_src, log_mass_tgt, potential_tgt, support, counts):
    n_src, n_tgt = lax.axis_size("src"), lax.axis_size("tgt")
    rows, feats, cells = source_feat.shape
    vmem = pl.BlockSpec(memory_space=pltpu.VMEM)
    f32 = jnp.float32
    dma = pltpu.SemaphoreType.DMA
    lists = jnp.transpose(support, (1, 2, 0))
    limits = counts.T
    return pl.pallas_call(
        functools.partial(sinkhorn_kernel, n_src, n_tgt, 4),
        out_shape=(
            jax.ShapeDtypeStruct((rows, cells), f32),
            jax.ShapeDtypeStruct((1, cells), f32),
        ),
        in_specs=[pl.BlockSpec(memory_space=pl.ANY)] * 7,
        out_specs=(vmem, vmem),
        scratch_shapes=[
            pltpu.VMEM(source_feat.shape, f32),
            pltpu.VMEM((rows, cells), f32),
            pltpu.VMEM(lists.shape, jnp.int32),
            pltpu.VMEM(limits.shape, jnp.int32),
            pltpu.VMEM((n_src, feats, cells), f32),
            pltpu.VMEM((n_src, cells), f32),
            pltpu.VMEM((n_src, cells), f32),
            pltpu.VMEM((rows * cells, 6 * feats), jnp.bfloat16),
            pltpu.VMEM((n_src, rows * cells, cells), f32),
            pltpu.VMEM((cells, cells), f32),
            pltpu.VMEM((rows, cells), f32),
            pltpu.VMEM((cells, cells), f32),
            pltpu.VMEM((rows * cells, cells), f32),
            pltpu.VMEM((rows, cells), f32),
            pltpu.VMEM((2 * rows, cells), f32),
            pltpu.VMEM((n_tgt, 2 * rows, cells), f32),
            pltpu.VMEM((n_src, 2, cells), f32),
            pltpu.VMEM((n_src, 2, cells), f32),
            dma((7,)),
            dma((3, n_src)),
            dma((3, n_src)),
            dma((n_tgt,)),
            dma((n_tgt,)),
            dma((n_src,)),
            dma((n_src,)),
        ],
        compiler_params=pltpu.CompilerParams(
            collective_id=0, has_side_effects=True, vmem_limit_bytes=60 * 1024 * 1024
        ),
        name="sinkhorn",
    )(source_feat, target_feat, log_mass_src, log_mass_tgt, potential_tgt, lists, limits)


def per_device(
    source_feat, target_feat, log_mass_src, log_mass_tgt, potential_tgt, support, counts
):
    rows, feats, cells = source_feat.shape
    n_src = lax.axis_size("src")
    dense = 4 * n_src * rows * cells * cells
    fits = (
        dense <= DENSE_BYTES
        and target_feat.shape[0] == 1
        and cells % 128 == 0
        and n_src * rows <= cells
        and rows % 8 == 0
        and not n_src & (n_src - 1)
        and 2 * feats == cells
        and n_src % 8 == 0
        and rows % 8 == 0
    )
    path = dense_path if fits else general_path
    return path(
        source_feat, target_feat, log_mass_src, log_mass_tgt, potential_tgt, support, counts
    )


def solution(mesh):
    in_specs = (
        P(("grp", "src"), None, None),
        P(("grp", "src", "tgt"), None, None),
        P(("grp", "src"), None),
        P(("grp", "src", "tgt"), None),
        P(("grp", "src", "tgt"), None),
        P(("grp", "src"), "tgt", None),
        P(("grp", "src"), "tgt"),
    )
    out_specs = (P(("grp", "src"), None), P(("grp", "src", "tgt"), None))
    return jax.shard_map(
        per_device, mesh=mesh, in_specs=in_specs, out_specs=out_specs, check_vma=False
    )
```

```python
import functools
import math

import jax
import jax.numpy as jnp
from jax import lax
from jax.experimental import pallas as pl
from jax.experimental.pallas import tpu as pltpu
from jax.sharding import PartitionSpec as P

entropic = 0.5
very_low = -1e30


def merged(part, axis, combine):
    gathered = jax.tree.map(lambda a: lax.all_gather(a, axis), part)

    def take(source):
        return jax.tree.map(lambda a: lax.dynamic_index_in_dim(a, source, 0, False), gathered)

    return lax.fori_loop(
        1, lax.axis_size(axis), lambda source, state: combine(state, take(source)), take(0)
    )


def cost_tiles(source_blk, source_sq, target_blk, target_sq):
    cross = jnp.einsum(
        "...fi,...fj->...ij", source_blk, target_blk, precision=lax.Precision.HIGHEST
    )
    return source_sq[..., :, None] + target_sq[..., None, :] - 2.0 * cross


def row_stats(cost, mass_tgt, poten_tgt, usable):
    scores = mass_tgt[..., None, :] + (poten_tgt[..., None, :] - cost) / entropic
    scores = jnp.where(usable[..., None, None], scores, very_low)
    peak = jnp.max(scores, axis=(1, 3))
    total = jnp.sum(jnp.exp(scores - peak[:, None, :, None]), axis=(1, 3))
    return (peak, total)


def column_stats(cost, mass_src, poten_src, usable):
    scores = mass_src[:, None, :, None] + (poten_src[:, None, :, None] - cost) / entropic
    peak = jnp.max(scores, axis=2)
    total = jnp.sum(jnp.exp(scores - peak[:, :, None, :]), axis=2)
    peak = jnp.where(usable[..., None], peak, very_low)
    total = jnp.where(usable[..., None], total, 0.0)
    return (peak, total)


def merge_pair(first_pair, second_pair):
    first_peak, first_total = first_pair
    second_peak, second_total = second_pair
    highest = jnp.maximum(first_peak, second_peak)
    summed = first_total * jnp.exp(first_peak - highest) + second_total * jnp.exp(
        second_peak - highest
    )
    return (highest, summed)


def segment_merge(peaks, totals, seg_ids, segments):
    best = jax.ops.segment_max(peaks, seg_ids, num_segments=segments + 1)
    best = jnp.maximum(best, very_low)
    summed = jax.ops.segment_sum(
        totals * jnp.exp(peaks - best[seg_ids]), seg_ids, num_segments=segments + 1
    )
    return (best[:segments], summed[:segments])


def general_path(
    source_feat, target_feat, log_mass_src, log_mass_tgt, potential_tgt, support, counts
):
    target_all, mass_all, poten_all = (
        lax.all_gather(target_feat, "src", axis=0, tiled=True),
        lax.all_gather(log_mass_tgt, "src", axis=0, tiled=True),
        lax.all_gather(potential_tgt, "src", axis=0, tiled=True),
    )
    blocks = target_all.shape[0]
    rows_here = source_feat.shape[0]
    slots_here = support.shape[2]
    cells = source_feat.shape[2]
    indices = support[:, 0, :]
    limits = counts[:, 0]
    usable = jnp.arange(slots_here, dtype=jnp.int32)[None, :] < limits[:, None]
    source_sq = jnp.sum(source_feat * source_feat, axis=1)
    target_sq = jnp.sum(target_all * target_all, axis=1)
    width = math.gcd(rows_here, 4)

    def grouped(array):
        return array.reshape((rows_here // width, width) + array.shape[1:])

    def row_pass(items):
        source_blk, source_nrm, ids_here, use_here = items
        cost = cost_tiles(
            source_blk[:, None], source_nrm[:, None], target_all[ids_here], target_sq[ids_here]
        )
        return row_stats(cost, mass_all[ids_here], poten_all[ids_here], use_here)

    peak, total = lax.map(
        row_pass, (grouped(source_feat), grouped(source_sq), grouped(indices), grouped(usable))
    )
    peak = peak.reshape(rows_here, cells)
    total = total.reshape(rows_here, cells)
    peak_all, total_all = merged((peak, total), "tgt", merge_pair)
    potential_src = -entropic * (peak_all + jnp.log(total_all))

    def column_pass(items):
        source_blk, source_nrm, mass_here, poten_here, ids_here, use_here = items
        cost = cost_tiles(
            source_blk[:, None], source_nrm[:, None], target_all[ids_here], target_sq[ids_here]
        )
        return column_stats(cost, mass_here, poten_here, use_here)

    peaks, totals = lax.map(
        column_pass,
        (
            grouped(source_feat),
            grouped(source_sq),
            grouped(log_mass_src),
            grouped(potential_src),
            grouped(indices),
            grouped(usable),
        ),
    )
    seg_ids = jnp.where(usable, indices, blocks).reshape(-1)
    best, summed = segment_merge(
        peaks.reshape(-1, cells), totals.reshape(-1, cells), seg_ids, blocks
    )
    share = blocks // lax.axis_size("src")
    own_start = lax.axis_index("src") * share
    highest = lax.pmax(best, "src")
    whole = lax.psum(summed * jnp.exp(best - highest), "src")
    own_peak = lax.dynamic_slice_in_dim(highest, own_start, share, 0)
    own_total = lax.dynamic_slice_in_dim(whole, own_start, share, 0)
    potential_new = -entropic * (own_peak + jnp.log(own_total))
    return (potential_src, potential_new)


LOG2E = 1.4426950408889634
LN2 = 0.6931471805599453
MESH = pl.DeviceIdType.MESH
DENSE_BYTES = 24 * 1024 * 1024


def split3(value):
    high = value.astype(jnp.bfloat16).astype(jnp.float32)
    rest = value - high
    mid = rest.astype(jnp.bfloat16).astype(jnp.float32)
    return high, mid, rest - mid


def partner(me, step, count):
    if count & (count - 1):
        return (me + step) % count
    met, bit = 0, 1
    while bit < count:
        met = met + bit * ((me // bit + step // bit) % 2)
        bit *= 2
    return met


def origin(me, step, count):
    if count & (count - 1):
        return (me - step + count) % count
    return partner(me, step, count)


def sinkhorn_kernel(
    n_src, n_tgt, group,
    x_hbm, y_hbm, lms_hbm, lmt_hbm, pt_hbm, sup_hbm, cnt_hbm,
    ps_ref, pn_ref,
    x_ref, lms_ref, sup_ref, cnt_ref,
    y_all, lm_all, pt_all, xt, scores, square, used, stat_col, shift,
    x_sq, stat_out, stat_in, col_out, col_in,
    local, y_send, y_recv, s_send, s_recv, c_send, c_recv,
):
    rows, feats, cells = x_ref.shape
    slots = sup_ref.shape[1]
    grp = lax.axis_index("grp")
    me = lax.axis_index("src")
    shard = lax.axis_index("tgt")

    barrier = pltpu.get_barrier_semaphore()
    for step in range(1, n_src):
        pl.semaphore_signal(
            barrier, inc=1, device_id=(grp, partner(me, step, n_src), shard), device_id_type=MESH
        )
    for step in range(1, n_tgt):
        pl.semaphore_signal(
            barrier, inc=1, device_id=(grp, me, (shard + step) % n_tgt), device_id_type=MESH
        )
    fetches = [
        pltpu.make_async_copy(here, there, local.at[index])
        for index, (here, there) in enumerate(
            (
                (x_hbm, x_ref),
                (sup_hbm, sup_ref),
                (cnt_hbm, cnt_ref),
                (lms_hbm, lms_ref),
                (y_hbm, y_all.at[pl.ds(me, 1)]),
                (lmt_hbm, lm_all.at[pl.ds(me, 1)]),
                (pt_hbm, pt_all.at[pl.ds(me, 1)]),
            )
        )
    ]
    for fetch in fetches:
        fetch.start()
    pl.semaphore_wait(barrier, n_src - 1 + n_tgt - 1)

    parts = ((y_hbm, y_all), (lmt_hbm, lm_all), (pt_hbm, pt_all))

    def target_copy(index, where, step, peer):
        mine, everyone = parts[index]
        return pltpu.make_async_remote_copy(
            src_ref=mine,
            dst_ref=everyone.at[pl.ds(where, 1)],
            send_sem=y_send.at[index, step],
            recv_sem=y_recv.at[index, where],
            device_id=(grp, peer, shard),
            device_id_type=MESH,
        )

    for step in range(1, n_src):
        peer = partner(me, step, n_src)
        for index in range(3):
            target_copy(index, me, step, peer).start()
    for fetch in fetches:
        fetch.wait()

    def prepare(row, carry):
        x = x_ref[row]
        x_sq[pl.ds(row, 1)] = jnp.sum(x * x, axis=0, keepdims=True)
        high, mid, low = split3(x * (4.0 * LOG2E))
        first = jnp.concatenate([high, mid], axis=0).T.astype(jnp.bfloat16)
        second = jnp.concatenate([low, high], axis=0).T.astype(jnp.bfloat16)
        here = pl.ds(row * cells, cells)
        xt[here, 0 : 2 * feats] = first
        xt[here, 2 * feats : 4 * feats] = first
        xt[here, 4 * feats : 6 * feats] = second
        return carry

    lax.fori_loop(0, rows, prepare, 0)

    limits = cnt_ref[...]
    names = lax.broadcasted_iota(jnp.int32, (n_src, rows), 0)
    joined = jnp.zeros((n_src, rows), jnp.bool_)
    for slot in range(slots):
        joined = joined | ((sup_ref[0, slot : slot + 1] == names) & (limits > slot))
    square[...] = jnp.zeros_like(square)
    square[0:n_src, 0:rows] = jnp.where(joined, 0.0, very_low)
    used[...] = square[...].T[:rows]
    row_lanes = lax.broadcasted_iota(jnp.int32, (rows, cells), 1)

    def operand(block):
        y = y_all[block]
        high, mid, low = split3(y)
        weights = jnp.concatenate([high, high, mid, mid, high, low], axis=0).astype(jnp.bfloat16)
        y_sq = jnp.sum(y * y, axis=0, keepdims=True)
        level = LOG2E * (
            lm_all[pl.ds(block, 1)] + 2.0 * pt_all[pl.ds(block, 1)] - 2.0 * y_sq
        )
        closed = jnp.sum(jnp.where(row_lanes == block, used[...], 0.0), axis=1, keepdims=True)
        return weights, level + closed

    lanes = lax.broadcasted_iota(jnp.int32, (cells, cells), 1)
    stat_col[...] = jnp.zeros_like(stat_col)

    def block_scores(turn, blocks):
        pairs = [operand(block) for block in blocks]
        weights = jnp.concatenate([pair[0] for pair in pairs], axis=1)
        filled = stat_col[...]
        for start in range(0, rows, group):
            here = slice(start * cells, (start + group) * cells)
            cross = jnp.dot(xt[here, :], weights, preferred_element_type=jnp.float32)
            for part in range(group):
                row = start + part
                tile = slice(row * cells, (row + 1) * cells)
                values = [
                    cross[part * cells : (part + 1) * cells, place * cells : (place + 1) * cells]
                    + pairs[place][1][row : row + 1]
                    for place in range(len(blocks))
                ]
                for block, value in zip(blocks, values):
                    scores[block, tile] = value
                peak = jnp.max(functools.reduce(jnp.maximum, values), axis=1, keepdims=True)
                total = functools.reduce(jnp.add, [jnp.exp2(value - peak) for value in values])
                total = jnp.sum(total, axis=1, keepdims=True)
                lane = turn * (2 * rows) + row
                filled = jnp.where(lanes == lane, peak, filled)
                filled = jnp.where(lanes == lane + rows, total, filled)
        stat_col[...] = filled

    def await_block(step):
        block = origin(me, step, n_src)
        for index in range(3):
            target_copy(index, block, step, block).wait_recv()
        return block

    block_scores(0, (me, await_block(1)))

    def arrival(index, carry):
        block_scores(index, (await_block(2 * index), await_block(2 * index + 1)))
        return carry

    lax.fori_loop(1, n_src // 2, arrival, 0)

    def joined_stats(first, second):
        highest = jnp.maximum(first[0], second[0])
        summed = first[1] * jnp.exp2(first[0] - highest) + second[1] * jnp.exp2(second[0] - highest)
        return highest, summed

    stats = stat_col[...].T
    turns = [
        (stats[2 * rows * turn :][:rows], stats[2 * rows * turn + rows :][:rows])
        for turn in range(n_src // 2)
    ]
    while len(turns) > 1:
        turns = [joined_stats(*turns[place : place + 2]) for place in range(0, len(turns), 2)]
    own_peak, own_total = turns[0]
    stat_out[0:rows] = own_peak
    stat_out[rows : 2 * rows] = own_total

    def stat_copy(where, step, peer):
        return pltpu.make_async_remote_copy(
            src_ref=stat_out,
            dst_ref=stat_in.at[where],
            send_sem=s_send.at[step],
            recv_sem=s_recv.at[where],
            device_id=(grp, me, peer),
            device_id_type=MESH,
        )

    for step in range(1, n_tgt):
        stat_copy(step, step, (shard + step) % n_tgt).start()
    for step in range(1, n_src):
        for index in range(3):
            target_copy(index, me, step, partner(me, step, n_src)).wait_send()
    for step in range(1, n_tgt):
        stat_copy(step, step, (shard + step) % n_tgt).wait_recv()
    peak, total = own_peak, own_total
    for step in range(1, n_tgt):
        other = (stat_in[step, 0:rows], stat_in[step, rows : 2 * rows])
        peak, total = joined_stats((peak, total), other)
    joint = peak + jnp.log(total) * LOG2E
    ps_ref[...] = x_sq[...] - (entropic * LN2) * joint
    offset = LOG2E * lms_ref[...] - joint
    offset = jnp.concatenate([offset, jnp.zeros((cells - rows, cells), jnp.float32)], axis=0).T
    for row in range(rows):
        shift[row * cells : (row + 1) * cells] = jnp.broadcast_to(
            offset[:, row : row + 1], (cells, cells)
        )

    many = 2 * group
    pieces = many * cells // 8
    lowest = jnp.full((8, cells), 4.0 * very_low, jnp.float32)
    nothing = jnp.zeros((8, cells), jnp.float32)

    def find(block, here, best):
        value = scores[block, here] + shift[here]
        return jnp.maximum(best, jnp.max(value.reshape(pieces, 8, cells), axis=0))

    def add(block, here, best, summed):
        value = jnp.exp2(scores[block, here] + shift[here] - best)
        return summed + jnp.sum(value.reshape(pieces, 8, cells), axis=0)

    def span(index):
        return pl.ds(index * many * cells, many * cells)

    def whole_column(summed):
        return jnp.sum(summed, axis=0, keepdims=True)

    def peak_of(best):
        return jnp.max(best, axis=0, keepdims=True)

    def column_copy(dest, where, step):
        return pltpu.make_async_remote_copy(
            src_ref=col_out.at[dest],
            dst_ref=col_in.at[where],
            send_sem=c_send.at[step],
            recv_sem=c_recv.at[where],
            device_id=(grp, dest, shard),
            device_id_type=MESH,
        )

    def send_column(index, best):
        step = n_src - 1 - index
        block = partner(me, step, n_src)
        following = partner(me, step - 1, n_src)
        summed, later = nothing, lowest
        for part in range(rows // many):
            summed = add(block, span(part), best, summed)
            later = find(following, span(part), later)
        col_out[block, 0:1] = best
        col_out[block, 1:2] = whole_column(summed)
        column_copy(block, me, step).start()
        return peak_of(later)

    farthest = partner(me, n_src - 1, n_src)
    best = lowest
    for part in range(rows // many):
        best = find(farthest, span(part), best)
    best = lax.fori_loop(0, n_src - 1, send_column, peak_of(best))
    summed = nothing
    for part in range(rows // many):
        summed = add(me, span(part), best, summed)
    summed = whole_column(summed)
    col_in[me, 0:1] = best
    col_in[me, 1:2] = summed
    for step in range(1, n_src):
        sender = origin(me, step, n_src)
        column_copy(sender, sender, step).wait_recv()
    peaks = col_in[:, 0, :]
    totals = col_in[:, 1, :]
    highest = jnp.max(peaks, axis=0, keepdims=True)
    whole = jnp.sum(totals * jnp.exp2(peaks - highest), axis=0, keepdims=True)
    pn_ref[...] = (
        pt_all[pl.ds(me, 1)]
        + entropic * lm_all[pl.ds(me, 1)]
        - (entropic * LN2) * (highest + jnp.log(whole) * LOG2E)
    )
    for step in range(1, n_tgt):
        stat_copy(step, step, (shard + step) % n_tgt).wait_send()
    for step in range(1, n_src):
        column_copy(partner(me, step, n_src), me, step).wait_send()


def dense_path(source_feat, target_feat, log_mass_src, log_mass_tgt, potential_tgt, support, counts):
    n_src, n_tgt = lax.axis_size("src"), lax.axis_size("tgt")
    rows, feats, cells = source_feat.shape
    vmem = pl.BlockSpec(memory_space=pltpu.VMEM)
    f32 = jnp.float32
    dma = pltpu.SemaphoreType.DMA
    lists = jnp.transpose(support, (1, 2, 0))
    limits = counts.T
    operands = [
        pltpu.with_memory_space_constraint(array, pltpu.HBM)
        for array in (
            source_feat, target_feat, log_mass_src, log_mass_tgt, potential_tgt, lists, limits
        )
    ]
    return pl.pallas_call(
        functools.partial(sinkhorn_kernel, n_src, n_tgt, 4),
        out_shape=(
            jax.ShapeDtypeStruct((rows, cells), f32),
            jax.ShapeDtypeStruct((1, cells), f32),
        ),
        in_specs=[pl.BlockSpec(memory_space=pltpu.HBM)] * 7,
        out_specs=(vmem, vmem),
        scratch_shapes=[
            pltpu.VMEM(source_feat.shape, f32),
            pltpu.VMEM((rows, cells), f32),
            pltpu.VMEM(lists.shape, jnp.int32),
            pltpu.VMEM(limits.shape, jnp.int32),
            pltpu.VMEM((n_src, feats, cells), f32),
            pltpu.VMEM((n_src, cells), f32),
            pltpu.VMEM((n_src, cells), f32),
            pltpu.VMEM((rows * cells, 6 * feats), jnp.bfloat16),
            pltpu.VMEM((n_src, rows * cells, cells), f32),
            pltpu.VMEM((cells, cells), f32),
            pltpu.VMEM((rows, cells), f32),
            pltpu.VMEM((cells, cells), f32),
            pltpu.VMEM((rows * cells, cells), f32),
            pltpu.VMEM((rows, cells), f32),
            pltpu.VMEM((2 * rows, cells), f32),
            pltpu.VMEM((n_tgt, 2 * rows, cells), f32),
            pltpu.VMEM((n_src, 2, cells), f32),
            pltpu.VMEM((n_src, 2, cells), f32),
            dma((7,)),
            dma((3, n_src)),
            dma((3, n_src)),
            dma((n_tgt,)),
            dma((n_tgt,)),
            dma((n_src,)),
            dma((n_src,)),
        ],
        compiler_params=pltpu.CompilerParams(
            collective_id=0, has_side_effects=True, vmem_limit_bytes=32 * 1024 * 1024
        ),
        name="sinkhorn",
    )(*operands)


def per_device(
    source_feat, target_feat, log_mass_src, log_mass_tgt, potential_tgt, support, counts
):
    rows, feats, cells = source_feat.shape
    n_src = lax.axis_size("src")
    dense = 4 * n_src * rows * cells * cells
    fits = (
        dense <= DENSE_BYTES
        and target_feat.shape[0] == 1
        and cells % 128 == 0
        and n_src * rows <= cells
        and rows % 8 == 0
        and not (n_src // 2) & (n_src // 2 - 1)
        and 2 * feats == cells
        and n_src % 8 == 0
        and rows % 8 == 0
    )
    path = dense_path if fits else general_path
    return path(
        source_feat, target_feat, log_mass_src, log_mass_tgt, potential_tgt, support, counts
    )


def solution(mesh):
    in_specs = (
        P(("grp", "src"), None, None),
        P(("grp", "src", "tgt"), None, None),
        P(("grp", "src"), None),
        P(("grp", "src", "tgt"), None),
        P(("grp", "src", "tgt"), None),
        P(("grp", "src"), "tgt", None),
        P(("grp", "src"), "tgt"),
    )
    out_specs = (P(("grp", "src"), None), P(("grp", "src", "tgt"), None))
    return jax.shard_map(
        per_device, mesh=mesh, in_specs=in_specs, out_specs=out_specs, check_vma=False
    )
```
